256 devices in a mesh: rad: 8 (over z_hi, core), azi: 32 (over y, z_lo, x).
Axes of the slice: x: 4, y: 4, z: 8 (z_hi: 4, z_lo: 2; z = z_hi * 2 + z_lo), core: 2. Of those that a mesh axis runs over, the one named last changes fastest.
Arguments:
- density: float32 [4, 256, 16384], P(None, 'rad', 'azi'), may hold values from -6 to 6
- radial_velocity: float32 [4, 256, 16384], P(None, 'rad', 'azi'), may hold values from -6 to 6
- azimuthal_velocity: float32 [4, 256, 16384], P(None, 'rad', 'azi'), may hold values from -6 to 6
- cycle_shift: int32 [256], P('rad'), may hold values from 0 to 16383
- remainder: float32 [256], P('rad'), may hold values from 0 to 1
- kernel: bfloat16 [2048, 256, 256], P(('rad', 'azi')), may hold values from -0.375 to 0.375
Outputs:
- density_next: float32 [4, 256, 16384], P(None, 'rad', 'azi')
- radial_next: float32 [4, 256, 16384], P(None, 'rad', 'azi')
- azimuthal_next: float32 [4, 256, 16384], P(None, 'rad', 'azi')
- potential: float32 [256, 16384], P(('rad', 'azi'))
The draws below stay inside these ranges and needn't reach their ends.
All inputs are finite; a program needn't handle non-finite values.
Results may differ from the reference program's by a relative error of at most 0.0003.
The reference program's roundings to bfloat16 on the way (of `spectrum`) count: a program that leaves them out, or rounds other values in their place, can miss the bound.
Values may be sent and summed in bfloat16 or wider, within the bound.
A program may use at most 256 MiB of HBM per device.

```python
import jax
import jax.numpy as jnp
from jax import lax

NZ = 4
NPHI = 16384
MODES = 2048
NR = 256


def touch_ends(array, key, least, largest):
    extent = array.shape
    index_at = [jax.random.randint(jax.random.fold_in(key, axis), (), 0, extent[axis]) for axis in range(len(extent))]
    array = array.at[tuple(index_at)].set(least)
    longest = extent.index(max(extent))
    index_at[longest] = (index_at[longest] + 1) % extent[longest]
    return array.at[tuple(index_at)].set(largest)


def levels(stream_key, dims, split, low, high):
    loudness, own = 1.0, jax.random.fold_in(stream_key, 6)
    for dim, parts in split:
        steps = jnp.exp(jax.random.uniform(jax.random.fold_in(own, dim), (parts,), jnp.float32, low / len(split), high / len(split)))
        loudness = loudness * jnp.repeat(steps, dims[dim] // parts).reshape([-1 if axis == dim else 1 for axis in range(len(dims))])
    return loudness


def normal_values(key, extent, scale, bound, pieces=(), kind=jnp.bfloat16):
    entries = jax.random.normal(key, extent, jnp.float32) * scale
    if len(pieces) > 0:
        entries = levels(key, extent, pieces, -0.22, 0.18) * entries
    return jnp.clip(entries, min=-bound, max=bound).astype(kind)


def setup_inputs(seed: int = 0) -> dict:
    seeds = jax.random.split(jax.random.key(seed), 7)
    return {
        "density": normal_values(seeds[0], (NZ, NR, NPHI), 1.0, 6.0, ((1, 8), (2, 32)), jnp.float32),
        "radial_velocity": normal_values(seeds[1], (NZ, NR, NPHI), 1.0, 6.0, ((1, 8), (2, 32)), jnp.float32),
        "azimuthal_velocity": normal_values(seeds[2], (NZ, NR, NPHI), 1.0, 6.0, ((1, 8), (2, 32)), jnp.float32),
        "cycle_shift": touch_ends(jax.random.randint(seeds[3], (NR,), 0, NPHI), jax.random.fold_in(seeds[3], 1), 0, NPHI - 1).astype(jnp.int32),
        "remainder": jnp.clip(1.0 * jax.random.uniform(seeds[4], (NR,), jnp.float32) ** levels(seeds[4], (NR,), ((0, 8),), -0.2, 0.2), 0.0, 1.0),
        "kernel": normal_values(seeds[5], (MODES, NR, NR), NR ** -0.5, 0.375, ((0, 256),)),
    }


RADIAL_COURANT = 0.3
VISCOSITY = 0.08


def cycle_coeffs(first_row, row_count, cycle_total):
    cycle_index = first_row + lax.broadcasted_iota(jnp.int32, (row_count, 1), 0)
    radius = 1.0 + 4.0 * (cycle_index.astype(jnp.float32) + 0.5) / cycle_total
    return 0.3 / radius, 0.2 * radius ** -1.5, 0.05 * radius ** -1.5


def rates(padded, coeffs):
    courant, coriolis, epicycle = coeffs
    extended = jnp.concatenate([padded[:, :1], padded, padded[:, -1:]], axis=1)
    center = extended[:, 1:-1, 1:-1, 1:-1]
    rad_diff = 0.5 * (extended[:, 1:-1, 2:, 1:-1] - extended[:, 1:-1, :-2, 1:-1])
    azi_diff = 0.5 * (extended[:, 1:-1, 1:-1, 2:] - extended[:, 1:-1, 1:-1, :-2])
    spread = (extended[:, 2:, 1:-1, 1:-1] + extended[:, :-2, 1:-1, 1:-1]
              + extended[:, 1:-1, 2:, 1:-1] + extended[:, 1:-1, :-2, 1:-1]
              + extended[:, 1:-1, 1:-1, 2:] + extended[:, 1:-1, 1:-1, :-2] - 6.0 * center)
    change_rho = -(RADIAL_COURANT * rad_diff[1] + courant * azi_diff[2]) + VISCOSITY * spread[0]
    change_radial = coriolis * center[2] - RADIAL_COURANT * rad_diff[0] + VISCOSITY * spread[1]
    change_azimuthal = -epicycle * center[1] - courant * azi_diff[0] + VISCOSITY * spread[2]
    return jnp.stack([change_rho, change_radial, change_azimuthal]), center


def pad_fields(fields):
    padded = jnp.pad(fields, ((0, 0), (0, 0), (1, 1), (0, 0)), mode="edge")
    return jnp.pad(padded, ((0, 0), (0, 0), (0, 0), (1, 1)), mode="wrap")


def cubic_weights(remainder):
    moved = -remainder[:, None]
    w_next = moved * (moved + 1.0) * (moved + 2.0) / 6.0
    w_here = -(moved - 1.0) * (moved + 1.0) * (moved + 2.0) / 2.0
    w_prev = (moved - 1.0) * moved * (moved + 2.0) / 2.0
    w_prev_two = -(moved - 1.0) * moved * (moved + 1.0) / 6.0
    return w_next, w_here, w_prev, w_prev_two


def reference(density, radial_velocity, azimuthal_velocity, cycle_shift, remainder, kernel):
    fields = jnp.stack([density, radial_velocity, azimuthal_velocity])
    coeffs = cycle_coeffs(0, NR, NR)
    change, center = rates(pad_fields(fields), coeffs)
    section_one = fields + change
    change_two, center_two = rates(pad_fields(section_one), coeffs)
    hydro = 0.5 * fields + 0.5 * (section_one + change_two)
    rotated = jax.vmap(lambda one_cycle, amount: jnp.roll(one_cycle, amount, axis=-1),
                       in_axes=(2, 0), out_axes=2)(hydro, cycle_shift)
    w_next, w_here, w_prev, w_prev_two = cubic_weights(remainder)
    moved = (w_next * jnp.roll(rotated, -1, axis=3) + w_here * rotated
             + w_prev * jnp.roll(rotated, 1, axis=3) + w_prev_two * jnp.roll(rotated, 2, axis=3))
    surface = jnp.sum(moved[0], axis=0)
    transform = jnp.fft.rfft(surface, axis=-1)[:, :MODES]
    spectrum = jnp.stack([jnp.real(transform), jnp.imag(transform)]).astype(jnp.bfloat16)
    columns = jnp.moveaxis(spectrum, 2, 0)

    def one_mode(pair):
        matrix, column = pair
        return jnp.dot(column.astype(jnp.float32), matrix.astype(jnp.float32).T,
                       precision=lax.Precision.HIGHEST)

    mode_potential = lax.map(one_mode, (kernel, columns))
    complex_modes = lax.complex(mode_potential[:, 0, :], mode_potential[:, 1, :]).T
    complex_modes = jnp.pad(complex_modes, ((0, 0), (0, NPHI // 2 + 1 - MODES)))
    potential = jnp.fft.irfft(complex_modes, n=NPHI, axis=-1)
    return moved[0], moved[1], moved[2], potential
```

```python
import numpy as np

import jax
import jax.numpy as jnp
from jax import lax
from jax.experimental import pallas as pl
from jax.experimental.pallas import tpu as pltpu
from jax.sharding import PartitionSpec as P

NZ = 4
NPHI = 16384
MODES = 2048
NR = 256
RAD = 8
AZI = 32
SLAB = NR // RAD
SEG = NPHI // AZI
LANES = 128
QUADS = SEG // LANES
MEMBERS = 3 * NZ
ROWS = MEMBERS * QUADS
EXT_R = SLAB + 8
EXT_P = SEG + LANES
RADIAL_COURANT = 0.3
VISCOSITY = 0.08
HIGHEST = lax.Precision.HIGHEST
F32 = jnp.float32
MESH = pl.DeviceIdType.MESH


def tables():
    n = np.arange(128)
    turn = 2.0 * np.pi / 128 * (np.outer(n, n) % 128)
    first = np.concatenate([np.cos(turn), -np.sin(turn)], axis=0)
    last = np.concatenate([np.cos(turn), -np.sin(turn)], axis=1)
    small = 2.0 * np.pi / NPHI * np.outer(n, n)
    twiddle = np.concatenate([np.cos(small), np.sin(small)], axis=0)
    col = np.arange(256)
    half, ring, part = col // 128, col % 16 // 2, col % 2
    phi = 2.0 * np.pi / 128 * (np.outer(n, 2 * ring + half) % 128)
    cos, sin = np.cos(phi), np.sin(phi)
    real = part == 0
    straight = np.concatenate([np.where(real, cos, -sin), np.where(real, sin, cos)], axis=0)
    turned = np.concatenate([np.where(real, sin, cos), np.where(real, -cos, sin)], axis=0)
    real = real[:, None]
    back = np.concatenate(
        [np.where(real, cos.T, -sin.T), np.where(real, sin.T, cos.T)], axis=1
    )
    return [t.astype(np.float32) for t in (first, last, twiddle, straight, turned, back)]


def dot(left, right):
    return jnp.dot(left, right, precision=HIGHEST, preferred_element_type=F32)


def iota(shape, axis):
    return lax.broadcasted_iota(jnp.int32, shape, axis)


def wide(value, count):
    return jnp.concatenate([value] * count, axis=1)


def cubic_weights(remainder):
    moved = -remainder
    w_next = moved * (moved + 1.0) * (moved + 2.0) / 6.0
    w_here = -(moved - 1.0) * (moved + 1.0) * (moved + 2.0) / 2.0
    w_prev = (moved - 1.0) * moved * (moved + 2.0) / 2.0
    w_prev_two = -(moved - 1.0) * moved * (moved + 1.0) / 6.0
    return w_next, w_here, w_prev, w_prev_two


def rates(get, z, rows, coeffs):
    courant, coriolis, epicycle = coeffs
    below, above = max(z - 1, 0), min(z + 1, NZ - 1)
    center, ahead, rad_diff, azi_diff, spread = [], [], [], [], []
    for c in range(3):
        whole = get(c, z)
        inner = pltpu.roll(whole, 1, 0)[:rows]
        outer = pltpu.roll(whole, EXT_R - 1, 0)[:rows]
        mid = whole[:rows]
        prev = pltpu.roll(mid, 1, 1)
        following = pltpu.roll(mid, EXT_P - 1, 1)
        center.append(mid)
        rad_diff.append(outer - inner if c < 2 else None)
        azi_diff.append(following - prev if c != 1 else None)
        total = (get(c, below)[:rows] + get(c, above)[:rows]) + (inner + outer) + (prev + following)
        spread.append(VISCOSITY * (total - 6.0 * mid))
    half = 0.5 * RADIAL_COURANT
    change = (
        spread[0] - (half * rad_diff[1] + courant * azi_diff[2]),
        spread[1] + coriolis * center[2] - half * rad_diff[0],
        spread[2] - epicycle * center[1] - courant * azi_diff[0],
    )
    return change, center


def body(
    density, radial_velocity, azimuthal_velocity, shift, rest, kernel, first, last, twiddle, straight,
    turned, back, density_out, radial_out, azimuthal_out, potential,
    ext, sect, coef, weight, row_send, row_in, tile_in, col_send, col_in, move_out, cycle_in, cycle_out,
    move_in, total, surf_out, surf_in, spec_out, spec_in, modes_out, modes_in, pot_out, pot_in, back_out,
    back_in, kern, t_first, t_last, t_twiddle, t_straight, t_turned, t_back,
    local_sem, halo_send, halo_recv, send_sem, recv_sem,
):
    rad, azi = lax.axis_index("rad"), lax.axis_index("azi")
    outer, inner = lax.rem(rad + 1, RAD), lax.rem(rad + RAD - 1, RAD)
    right, left = lax.rem(azi + 1, AZI), lax.rem(azi + AZI - 1, AZI)

    loads = [
        pltpu.make_async_copy(src, ext.at[pl.ds(NZ * c, NZ), pl.ds(0, SLAB), pl.ds(0, SEG)], local_sem.at[c])
        for c, src in enumerate((density, radial_velocity, azimuthal_velocity))
    ]
    for n, (src, dst) in enumerate(
        (
            (first, t_first), (twiddle, t_twiddle), (straight, t_straight), (turned, t_turned),
            (kernel, kern), (back, t_back), (last, t_last),
        )
    ):
        loads.append(pltpu.make_async_copy(src, dst, local_sem.at[3 + n]))
    for load in loads:
        load.start()

    col_in[...] = jnp.zeros(col_in.shape, F32)
    barrier = pltpu.get_barrier_semaphore()

    def greet_azi(step, carry):
        pl.semaphore_signal(
            barrier, inc=1, device_id={"rad": rad, "azi": lax.rem(azi + step, AZI)}, device_id_type=MESH
        )
        return carry

    def greet_rad(step, carry):
        pl.semaphore_signal(
            barrier, inc=1, device_id={"rad": lax.rem(rad + step, RAD), "azi": azi}, device_id_type=MESH
        )
        return carry

    for r_to in (outer, inner):
        for a_to in (right, left):
            pl.semaphore_signal(barrier, inc=1, device_id={"rad": r_to, "azi": a_to}, device_id_type=MESH)
    lax.fori_loop(1, AZI, greet_azi, 0)
    lax.fori_loop(1, RAD, greet_rad, 0)

    row = iota((EXT_R, LANES), 0)
    cycle = SLAB * rad + jnp.where(row < SLAB + 4, row, row - EXT_R)
    radius = 1.0 + 4.0 * (cycle.astype(F32) + 0.5) / NR
    steep = 1.0 / (radius * jnp.sqrt(radius))
    coef[0] = 0.15 / radius
    coef[1] = 0.2 * steep
    coef[2] = 0.05 * steep
    block_row = iota((8, LANES), 0)
    for block in range(SLAB // 8):
        fraction = jnp.zeros((8, LANES), F32)
        for n in range(8):
            fraction = jnp.where(block_row == n, rest[8 * block + n], fraction)
        for n, value in enumerate(cubic_weights(fraction)):
            weight[n, pl.ds(8 * block, 8), :] = value
    ext[:, pl.ds(SLAB, 8), :] = jnp.zeros((MEMBERS, 8, EXT_P), F32)

    for load in loads[:3]:
        load.wait()
    lane_tile = iota((SLAB, LANES), 1)
    mixed = []
    for m in range(MEMBERS):
        low = ext[m, pl.ds(0, SLAB), pl.ds(0, LANES)]
        high = ext[m, pl.ds(0, SLAB), pl.ds(SEG - LANES, LANES)]
        edge = jnp.where(lane_tile < LANES // 2, low, high)
        mixed.append(edge)
        for n, at in enumerate((SLAB - 2, 0)):
            row_send[n, pl.ds(2 * m, 2), pl.ds(0, SEG)] = ext[m, pl.ds(at, 2), pl.ds(0, SEG)]
            row_send[n, pl.ds(2 * m, 2), pl.ds(SEG, LANES)] = edge[at : at + 2]
    columns = jnp.concatenate(mixed, axis=0).T
    col_send[0] = columns[LANES - 8 :]
    col_send[1] = columns[:8]

    pl.semaphore_wait(barrier, AZI - 1 + RAD - 1 + 4)

    def halo(n, src, dst, r_to, a_to):
        return pltpu.make_async_remote_copy(
            src_ref=src, dst_ref=dst, send_sem=halo_send.at[n], recv_sem=halo_recv.at[n],
            device_id={"rad": r_to, "azi": a_to}, device_id_type=MESH,
        )

    plain, corner = pl.ds(0, SEG), pl.ds(SEG, LANES)
    halos = [
        halo(0, row_send.at[0, :, plain], row_in.at[0], outer, azi),
        halo(1, row_send.at[1, :, plain], row_in.at[1], inner, azi),
        halo(2, col_send.at[0], col_in.at[pl.ds(LANES - 8, 8)], rad, right),
        halo(3, col_send.at[1], col_in.at[pl.ds(0, 8)], rad, left),
        halo(4, row_send.at[0, :, corner], tile_in.at[0], outer, right),
        halo(5, row_send.at[0, :, corner], tile_in.at[1], outer, left),
        halo(6, row_send.at[1, :, corner], tile_in.at[2], inner, right),
        halo(7, row_send.at[1, :, corner], tile_in.at[3], inner, left),
    ]
    for one in halos:
        one.start()
    my_shift = shift[azi]
    col = iota((16, 256), 1)
    mode = 256 * (col % 16 // 2) + 128 * (col // 128) + 8 * iota((16, 256), 0) + col // 16 % 8
    phase = (2.0 * np.pi / NPHI) * ((mode * my_shift) & (NPHI - 1)).astype(F32)
    phase_cos, phase_sin = jnp.cos(phase), -jnp.sin(phase)
    for one in halos:
        one.wait_recv()

    sides = col_in[...].T
    lane_two = iota((2, LANES), 1)
    for m in range(MEMBERS):
        ext[m, pl.ds(0, SLAB), pl.ds(SEG, LANES)] = sides[SLAB * m : SLAB * (m + 1)]
    for m in range(MEMBERS):
        pair = pl.ds(2 * m, 2)
        for n, (at, edge_at, at_edge) in enumerate(
            ((EXT_R - 2, 0, rad == 0), (SLAB, SLAB - 1, rad == RAD - 1))
        ):
            edge = ext[m, pl.ds(edge_at, 1), :]
            far = jnp.where(lane_two < LANES // 2, tile_in[2 * n + 1, pair, :], tile_in[2 * n, pair, :])
            got = jnp.concatenate([row_in[n, pair, :], far], axis=1)
            ext[m, pl.ds(at, 2), :] = jnp.where(at_edge, jnp.broadcast_to(edge, (2, EXT_P)), got)

    coeffs = [wide(coef[n], EXT_P // LANES) for n in range(3)]
    for z in range(NZ):
        change, center = rates(lambda c, zz: ext[NZ * c + zz], z, EXT_R, coeffs)
        for c in range(3):
            sect[NZ * c + z] = center[c] + change[c]
    for m in range(MEMBERS):
        top = sect[m, pl.ds(0, 1), :]
        sect[m, pl.ds(EXT_R - 1, 1), :] = jnp.where(rad == 0, top, sect[m, pl.ds(EXT_R - 1, 1), :])
        low = sect[m, pl.ds(SLAB - 1, 1), :]
        sect[m, pl.ds(SLAB, 1), :] = jnp.where(rad == RAD - 1, low, sect[m, pl.ds(SLAB, 1), :])
    coeffs = [wide(coef[n, pl.ds(0, SLAB), :], EXT_P // LANES) for n in range(3)]
    weights = [weight[n] for n in range(4)]
    for z in range(NZ):
        change, center = rates(lambda c, zz: sect[NZ * c + zz], z, SLAB, coeffs)
        for c in range(3):
            m = NZ * c + z
            hydro = 0.5 * ext[m, pl.ds(0, SLAB), :] + 0.5 * (center[c] + change[c])
            ahead = pltpu.roll(hydro, EXT_P - 1, 1)
            behind = pltpu.roll(hydro, 1, 1)
            behind_two = pltpu.roll(hydro, 2, 1)
            for quad in range(QUADS):
                lanes = slice(LANES * quad, LANES * (quad + 1))
                moved = (
                    weights[0] * ahead[:, lanes] + weights[1] * hydro[:, lanes]
                    + weights[2] * behind[:, lanes] + weights[3] * behind_two[:, lanes]
                )
                for block in range(SLAB // 8):
                    move_out[pl.ds(8 * ROWS * block + MEMBERS * quad + m, 8, stride=ROWS), :] = moved[
                        8 * block : 8 * block + 8
                    ]
                if c == 0:
                    if z == 0:
                        total[:, lanes] = moved
                    else:
                        total[:, lanes] += moved
    for n in range(SLAB):
        for quad in range(QUADS):
            surf_out[n, quad, :] = total[n, LANES * quad : LANES * (quad + 1)]

    def to_azi(n, src, dst, step):
        return pltpu.make_async_remote_copy(
            src_ref=src, dst_ref=dst, send_sem=send_sem.at[n], recv_sem=recv_sem.at[n],
            device_id={"rad": rad, "azi": lax.rem(azi + step, AZI)}, device_id_type=MESH,
        )

    def to_rad(n, src, dst, step):
        return pltpu.make_async_remote_copy(
            src_ref=src, dst_ref=dst, send_sem=send_sem.at[n], recv_sem=recv_sem.at[n],
            device_id={"rad": lax.rem(rad + step, RAD), "azi": azi}, device_id_type=MESH,
        )

    def every(count, make):
        def one(step, carry):
            make(step).start()
            return carry

        lax.fori_loop(1, count, one, 0)

    def rows(index, size=ROWS):
        return pl.ds(pl.multiple_of(index * size, 8), size)

    def wait_all(n, ref, sem):
        pltpu.make_async_copy(ref, ref, sem.at[n]).wait()

    def target(step):
        return lax.rem(azi + step, AZI)

    def ring(step):
        return lax.rem(rad + step, RAD)

    every(AZI, lambda s: to_azi(0, surf_out.at[target(s)], surf_in.at[azi], s))
    surf_in[azi] = surf_out[azi]
    every(AZI, lambda s: to_azi(1, move_out.at[rows(target(s))], cycle_in.at[rows(azi)], s))
    cycle_in[rows(azi), :] = move_out[rows(azi), :]

    for load in loads[3:7]:
        load.wait()
    wait_all(0, surf_in.at[pl.ds(1, AZI - 1)], recv_sem)
    lines = surf_in[...].reshape(128, 128)
    halves = dot(t_first[...], lines)
    turn_cos, turn_sin = t_twiddle[:128], t_twiddle[128:]
    real, imag = halves[:128], halves[128:]
    joined = jnp.concatenate([real * turn_cos + imag * turn_sin, imag * turn_cos - real * turn_sin], axis=1)
    own = iota((128, 256), 0) % 8 == iota((128, 256), 1) // 16 % 8
    pick = (iota((16, 128), 1) // 8 == iota((16, 128), 0)).astype(F32)
    plain_modes = dot(pick, jnp.where(own, dot(joined, t_straight[...]), 0.0))
    turned_modes = dot(pick, jnp.where(own, dot(joined, t_turned[...]), 0.0))
    spectrum = (plain_modes * phase_cos + turned_modes * phase_sin).astype(jnp.bfloat16).astype(F32)
    for h in range(2):
        for q in range(16):
            spec_out[16 * h + q, 0, :] = spectrum[q, 128 * h : 128 * (h + 1)]
    every(AZI, lambda s: to_azi(2, spec_out.at[target(s)], spec_in.at[azi], s))
    spec_in[azi] = spec_out[azi]

    wait_all(1, cycle_in.at[pl.ds(0, ROWS * (AZI - 1))], recv_sem)
    cycle_in[pl.ds(ROWS * AZI, ROWS), :] = cycle_in[pl.ds(0, ROWS), :]
    turn_rows, turn_lanes = my_shift // LANES, my_shift % LANES
    lane = iota((ROWS, LANES), 1)

    def rotated(segment):
        start = lax.rem(QUADS * segment + LANES - 1 - turn_rows + LANES, LANES) * MEMBERS
        here = cycle_in[pl.ds(start + MEMBERS, ROWS), :]
        before = cycle_in[pl.ds(start, ROWS), :]
        return pltpu.roll(jnp.where(lane < LANES - turn_lanes, here, before), turn_lanes, 1)

    def rotate_and_send(step, carry):
        segment = target(step)
        cycle_out[rows(segment), :] = rotated(segment)
        to_azi(3, cycle_out.at[rows(segment)], move_in.at[rows(azi)], step).start()
        return carry

    lax.fori_loop(1, AZI, rotate_and_send, 0)
    move_in[rows(azi), :] = rotated(azi)

    wait_all(2, spec_in.at[pl.ds(1, AZI - 1)], recv_sem)
    modes_out[...] = spec_in[:, 0, :].astype(jnp.bfloat16)
    every(RAD, lambda s: to_rad(4, modes_out, modes_in.at[rad], s))
    modes_in[rad] = modes_out[...]
    wait_all(4, modes_in.at[pl.ds(1, RAD - 1)], recv_sem)
    columns = modes_in[...].reshape(NR, 128)
    loads[7].wait()
    out_lane = iota((NR, 128), 1)
    mine = out_lane % 16 // 2 == rad
    mode_potential = jnp.zeros((NR, 128), F32)
    for k in range(8):
        product = jnp.dot(kern[k], columns, preferred_element_type=F32)
        mode_potential = jnp.where(mine & (out_lane // 16 == k), product, mode_potential)
    pot_out[...] = mode_potential
    every(RAD, lambda s: to_rad(5, pot_out.at[rows(ring(s), SLAB)], pot_in.at[rad], s))
    pot_in[rad] = pot_out[rows(rad, SLAB), :]
    wait_all(5, pot_in.at[pl.ds(1, RAD - 1)], recv_sem)
    gathered = pot_in[0]
    for n in range(1, RAD):
        gathered = gathered + pot_in[n]
    for n in range(SLAB):
        back_out[n, 0, :] = gathered[n]
    every(AZI, lambda s: to_azi(6, back_out.at[target(s)], back_in.at[azi], s))
    back_in[azi] = back_out[azi]
    for load in loads[8:]:
        load.wait()
    wait_all(6, back_in.at[pl.ds(1, AZI - 1)], recv_sem)
    values = back_in[:, 0, :]
    values = jnp.concatenate([values[:16], values[16:]], axis=1)
    spread = (iota((128, 16), 0) // 8 == iota((128, 16), 1)).astype(F32)
    zero_mode = (iota((128, 256), 0) == 0) & (iota((128, 256), 1) < 2)
    values = jnp.where(own, dot(spread, values) * jnp.where(zero_mode, 1.0 / NPHI, 2.0 / NPHI), 0.0)
    pieces = dot(values, t_back[...])
    real, imag = pieces[:, :128], pieces[:, 128:]
    joined = jnp.concatenate([real * turn_cos - imag * turn_sin, real * turn_sin + imag * turn_cos], axis=0)
    potential[...] = dot(t_last[...], joined)

    wait_all(3, move_in.at[pl.ds(0, ROWS * (AZI - 1))], recv_sem)
    for c, out in enumerate((density_out, radial_out, azimuthal_out)):
        for z in range(NZ):
            for quad in range(QUADS):
                for block in range(SLAB // 8):
                    at = 8 * ROWS * block + MEMBERS * quad + NZ * c + z
                    out[z, pl.ds(8 * block, 8), pl.ds(LANES * quad, LANES)] = move_in[
                        pl.ds(at, 8, stride=ROWS), :
                    ]

    for one in halos:
        one.wait_send()
    wait_all(0, surf_in.at[pl.ds(1, AZI - 1)], send_sem)
    wait_all(1, cycle_in.at[pl.ds(0, ROWS * (AZI - 1))], send_sem)
    wait_all(2, spec_in.at[pl.ds(1, AZI - 1)], send_sem)
    wait_all(3, move_in.at[pl.ds(0, ROWS * (AZI - 1))], send_sem)
    wait_all(4, modes_in.at[pl.ds(1, RAD - 1)], send_sem)
    wait_all(5, pot_in.at[pl.ds(1, RAD - 1)], send_sem)
    wait_all(6, back_in.at[pl.ds(1, AZI - 1)], send_sem)


def step(density, radial_velocity, azimuthal_velocity, cycle_shift, remainder, kernel):
    whole = pl.BlockSpec(memory_space=pltpu.VMEM)
    away = pl.BlockSpec(memory_space=pl.ANY)
    scalars = pl.BlockSpec(memory_space=pltpu.SMEM)
    block = jax.ShapeDtypeStruct((NZ, SLAB, SEG), F32)
    moves = pltpu.VMEM((ROWS * AZI, LANES), F32)
    single = pltpu.VMEM((AZI, 1, LANES), F32)
    *moved, potential = pl.pallas_call(
        body,
        name="disc_step",
        out_shape=[block, block, block, jax.ShapeDtypeStruct((128, 128), F32)],
        in_specs=[away] * 3 + [scalars] * 2 + [away] * 7,
        out_specs=[whole] * 4,
        scratch_shapes=[
            pltpu.VMEM((MEMBERS, EXT_R, EXT_P), F32),
            pltpu.VMEM((MEMBERS, EXT_R, EXT_P), F32),
            pltpu.VMEM((3, EXT_R, LANES), F32),
            pltpu.VMEM((4, SLAB, LANES), F32),
            pltpu.VMEM((2, 2 * MEMBERS, EXT_P), F32),
            pltpu.VMEM((2, 2 * MEMBERS, SEG), F32),
            pltpu.VMEM((4, 2 * MEMBERS, LANES), F32),
            pltpu.VMEM((2, 8, MEMBERS * SLAB), F32),
            pltpu.VMEM((LANES, MEMBERS * SLAB), F32),
            moves,
            pltpu.VMEM((ROWS * (AZI + 1), LANES), F32),
            moves,
            moves,
            pltpu.VMEM((SLAB, SEG), F32),
            pltpu.VMEM((AZI, QUADS, LANES), F32),
            pltpu.VMEM((AZI, QUADS, LANES), F32),
            single,
            single,
            pltpu.VMEM((AZI, LANES), jnp.bfloat16),
            pltpu.VMEM((RAD, AZI, LANES), jnp.bfloat16),
            pltpu.VMEM((NR, LANES), F32),
            pltpu.VMEM((RAD, AZI, LANES), F32),
            single,
            single,
            pltpu.VMEM((8, NR, NR), jnp.bfloat16),
            pltpu.VMEM((256, 128), F32),
            pltpu.VMEM((128, 256), F32),
            pltpu.VMEM((256, 128), F32),
            pltpu.VMEM((256, 256), F32),
            pltpu.VMEM((256, 256), F32),
            pltpu.VMEM((256, 256), F32),
            pltpu.SemaphoreType.DMA((10,)),
            pltpu.SemaphoreType.DMA((8,)),
            pltpu.SemaphoreType.DMA((8,)),
            pltpu.SemaphoreType.DMA((7,)),
            pltpu.SemaphoreType.DMA((7,)),
        ],
        compiler_params=pltpu.CompilerParams(
            collective_id=0, has_side_effects=True, vmem_limit_bytes=40 * 1024 * 1024
        ),
    )(
        density, radial_velocity, azimuthal_velocity, cycle_shift, remainder, kernel,
        *[jnp.asarray(t) for t in tables()],
    )
    return *moved, potential.reshape(1, NPHI)


def solution(mesh):
    field = P(None, "rad", "azi")
    both = P(("rad", "azi"), None)
    return jax.shard_map(
        step,
        mesh=mesh,
        in_specs=(field, field, field, P("rad"), P("rad"), P(("rad", "azi"), None, None)),
        out_specs=(field, field, field, both),
        check_vma=False,
    )
```

```python
import numpy as np

import jax
import jax.numpy as jnp
from jax import lax
from jax.experimental import pallas as pl
from jax.experimental.pallas import tpu as pltpu
from jax.sharding import PartitionSpec as P

NZ = 4
NPHI = 16384
MODES = 2048
NR = 256
RAD = 8
AZI = 32
SLAB = NR // RAD
SEG = NPHI // AZI
LANES = 128
QUADS = SEG // LANES
MEMBERS = 3 * NZ
ROWS = MEMBERS * QUADS
EXT_R = SLAB + 8
EXT_P = SEG + LANES
RADIAL_COURANT = 0.3
VISCOSITY = 0.08
HIGHEST = lax.Precision.HIGHEST
F32 = jnp.float32
MESH = pl.DeviceIdType.MESH


def tables():
    n = np.arange(128)
    turn = 2.0 * np.pi / 128 * (np.outer(n, n) % 128)
    first = np.concatenate([np.cos(turn), -np.sin(turn)], axis=0)
    last = np.concatenate([np.cos(turn), -np.sin(turn)], axis=1)
    small = 2.0 * np.pi / NPHI * np.outer(n, n)
    twiddle = np.concatenate([np.cos(small), np.sin(small)], axis=0)
    col = np.arange(256)
    half, ring, part = col // 128, col % 128 // 16, col % 2
    phi = 2.0 * np.pi / 128 * (np.outer(n, 2 * ring + half) % 128)
    cos, sin = np.cos(phi), np.sin(phi)
    real = part == 0
    straight = np.concatenate([np.where(real, cos, -sin), np.where(real, sin, cos)], axis=0)
    real = real[:, None]
    back = np.concatenate(
        [np.where(real, cos.T, -sin.T), np.where(real, sin.T, cos.T)], axis=1
    )
    return [t.astype(np.float32) for t in (first, last, twiddle, straight, back)]


def dot(left, right):
    return jnp.dot(left, right, precision=HIGHEST, preferred_element_type=F32)


def iota(shape, axis):
    return lax.broadcasted_iota(jnp.int32, shape, axis)


def wide(value, count):
    return jnp.concatenate([value] * count, axis=1)


def cubic_weights(remainder):
    moved = -remainder
    w_next = moved * (moved + 1.0) * (moved + 2.0) / 6.0
    w_here = -(moved - 1.0) * (moved + 1.0) * (moved + 2.0) / 2.0
    w_prev = (moved - 1.0) * moved * (moved + 2.0) / 2.0
    w_prev_two = -(moved - 1.0) * moved * (moved + 1.0) / 6.0
    return w_next, w_here, w_prev, w_prev_two


def rates(get, z, rows, coeffs):
    courant, coriolis, epicycle = coeffs
    below, above = max(z - 1, 0), min(z + 1, NZ - 1)
    center, ahead, rad_diff, azi_diff, spread = [], [], [], [], []
    for c in range(3):
        whole = get(c, z)
        inner = pltpu.roll(whole, 1, 0)[:rows]
        outer = pltpu.roll(whole, EXT_R - 1, 0)[:rows]
        mid = whole[:rows]
        prev = pltpu.roll(mid, 1, 1)
        following = pltpu.roll(mid, EXT_P - 1, 1)
        center.append(mid)
        rad_diff.append(outer - inner if c < 2 else None)
        azi_diff.append(following - prev if c != 1 else None)
        total = (get(c, below)[:rows] + get(c, above)[:rows]) + (inner + outer) + (prev + following)
        spread.append(VISCOSITY * (total - 6.0 * mid))
    half = 0.5 * RADIAL_COURANT
    change = (
        spread[0] - (half * rad_diff[1] + courant * azi_diff[2]),
        spread[1] + coriolis * center[2] - half * rad_diff[0],
        spread[2] - epicycle * center[1] - courant * azi_diff[0],
    )
    return change, center


def body(
    density, radial_velocity, azimuthal_velocity, shift_far, rest_far, kernel, first, last, twiddle, straight,
    back, moved_out, potential,
    ext, sect, coef, weight, row_send, row_in, tile_in, col_send, col_in, move_out, cycle_in, cycle_out,
    move_in, surf_out, surf_in, spec_out, spec_in, modes_out, modes_in, pot_out, pot_in, lines, back_out,
    back_in, kern, t_first, t_last, t_twiddle, t_straight, t_back,
    shift, rest, local_sem, halo_send, halo_recv, send_sem, recv_sem,
):
    rad, azi = lax.axis_index("rad"), lax.axis_index("azi")
    outer, inner = lax.rem(rad + 1, RAD), lax.rem(rad + RAD - 1, RAD)
    right, left = lax.rem(azi + 1, AZI), lax.rem(azi + AZI - 1, AZI)

    loads = [
        pltpu.make_async_copy(src, ext.at[pl.ds(NZ * c, NZ), pl.ds(0, SLAB), pl.ds(0, SEG)], local_sem.at[c])
        for c, src in enumerate((density, radial_velocity, azimuthal_velocity))
    ]
    for n, (src, dst) in enumerate(
        (
            (first, t_first), (twiddle, t_twiddle), (straight, t_straight),
            (kernel, kern), (back, t_back), (last, t_last), (shift_far, shift), (rest_far, rest),
        )
    ):
        loads.append(pltpu.make_async_copy(src, dst, local_sem.at[3 + n]))
    for load in loads:
        load.start()

    col_in[...] = jnp.zeros(col_in.shape, F32)
    barrier = pltpu.get_barrier_semaphore()

    def greet_azi(step, carry):
        pl.semaphore_signal(
            barrier, inc=1, device_id={"rad": rad, "azi": lax.rem(azi + step, AZI)}, device_id_type=MESH
        )
        return carry

    def greet_rad(step, carry):
        pl.semaphore_signal(
            barrier, inc=1, device_id={"rad": lax.rem(rad + step, RAD), "azi": azi}, device_id_type=MESH
        )
        return carry

    for r_to in (outer, inner):
        for a_to in (right, left):
            pl.semaphore_signal(barrier, inc=1, device_id={"rad": r_to, "azi": a_to}, device_id_type=MESH)
    lax.fori_loop(1, AZI, greet_azi, 0)
    lax.fori_loop(1, RAD, greet_rad, 0)

    row = iota((EXT_R, LANES), 0)
    cycle = SLAB * rad + jnp.where(row < SLAB + 4, row, row - EXT_R)
    radius = 1.0 + 4.0 * (cycle.astype(F32) + 0.5) / NR
    steep = 1.0 / (radius * jnp.sqrt(radius))
    coef[0] = 0.15 / radius
    coef[1] = 0.2 * steep
    coef[2] = 0.05 * steep
    for load in loads[9:]:
        load.wait()
    block_row = iota((8, LANES), 0)
    for block in range(SLAB // 8):
        fraction = jnp.zeros((8, LANES), F32)
        for n in range(8):
            fraction = jnp.where(block_row == n, rest[8 * block + n], fraction)
        for n, value in enumerate(cubic_weights(fraction)):
            weight[n, pl.ds(8 * block, 8), :] = value
    ext[:, pl.ds(SLAB, 8), :] = jnp.zeros((MEMBERS, 8, EXT_P), F32)

    for load in loads[:3]:
        load.wait()
    lane_tile = iota((SLAB, LANES), 1)
    mixed = []
    for m in range(MEMBERS):
        low = ext[m, pl.ds(0, SLAB), pl.ds(0, LANES)]
        high = ext[m, pl.ds(0, SLAB), pl.ds(SEG - LANES, LANES)]
        edge = jnp.where(lane_tile < LANES // 2, low, high)
        mixed.append(edge)
        for n, at in enumerate((SLAB - 2, 0)):
            row_send[n, pl.ds(2 * m, 2), pl.ds(0, SEG)] = ext[m, pl.ds(at, 2), pl.ds(0, SEG)]
            row_send[n, pl.ds(2 * m, 2), pl.ds(SEG, LANES)] = edge[at : at + 2]
    columns = jnp.concatenate(mixed, axis=0).T
    col_send[0] = columns[LANES - 8 :]
    col_send[1] = columns[:8]

    for c in range(3):
        heights = [ext[NZ * c + z, pl.ds(0, SLAB), pl.ds(0, SEG)] for z in range(NZ)]
        total = (heights[0] + heights[1]) + (heights[2] + heights[3])
        for n in range(SLAB):
            for quad in range(QUADS):
                surf_out[c, n, quad, :] = total[n, LANES * quad : LANES * (quad + 1)]

    pl.semaphore_wait(barrier, AZI - 1 + RAD - 1 + 4)

    def halo(n, src, dst, r_to, a_to):
        return pltpu.make_async_remote_copy(
            src_ref=src, dst_ref=dst, send_sem=halo_send.at[n], recv_sem=halo_recv.at[n],
            device_id={"rad": r_to, "azi": a_to}, device_id_type=MESH,
        )

    plain, corner = pl.ds(0, SEG), pl.ds(SEG, LANES)
    halos = [
        halo(0, row_send.at[0, :, plain], row_in.at[0], outer, azi),
        halo(1, row_send.at[1, :, plain], row_in.at[1], inner, azi),
        halo(2, col_send.at[0], col_in.at[pl.ds(LANES - 8, 8)], rad, right),
        halo(3, col_send.at[1], col_in.at[pl.ds(0, 8)], rad, left),
        halo(4, row_send.at[0, :, corner], tile_in.at[0], outer, right),
        halo(5, row_send.at[0, :, corner], tile_in.at[1], outer, left),
        halo(6, row_send.at[1, :, corner], tile_in.at[2], inner, right),
        halo(7, row_send.at[1, :, corner], tile_in.at[3], inner, left),
    ]
    for one in halos:
        one.start()
    finish = [one.wait_send for one in halos]
    def to_azi(n, src, dst, step):
        return pltpu.make_async_remote_copy(
            src_ref=src, dst_ref=dst, send_sem=send_sem.at[n], recv_sem=recv_sem.at[n],
            device_id={"rad": rad, "azi": lax.rem(azi + step, AZI)}, device_id_type=MESH,
        )

    def to_rad(n, src, dst, step):
        return pltpu.make_async_remote_copy(
            src_ref=src, dst_ref=dst, send_sem=send_sem.at[n], recv_sem=recv_sem.at[n],
            device_id={"rad": lax.rem(rad + step, RAD), "azi": azi}, device_id_type=MESH,
        )

    def every(count, make):
        def one(step, carry):
            make(step).start()
            return carry

        lax.fori_loop(1, count, one, 0)

    def rows(index, size=ROWS):
        return pl.ds(pl.multiple_of(index * size, 8), size)

    def wait_all(n, ref, sem):
        pltpu.make_async_copy(ref, ref, sem.at[n]).wait()

    def later(n, ref):
        finish.append(lambda: wait_all(n, ref, send_sem))

    def target(step):
        return lax.rem(azi + step, AZI)

    def ring(step):
        return lax.rem(rad + step, RAD)

    every(AZI, lambda s: to_azi(0, surf_out.at[:, target(s)], surf_in.at[:, azi], s))
    later(0, surf_in.at[:, pl.ds(1, AZI - 1)])
    for c in range(3):
        surf_in[c, azi] = surf_out[c, azi]

    for load in loads[3:6]:
        load.wait()
    wait_all(0, surf_in.at[:, pl.ds(1, AZI - 1)], recv_sem)
    sums = jnp.concatenate([surf_in[c].reshape(128, 128) for c in range(3)], axis=1)
    halves = dot(t_first[...], sums)
    joined = []
    for c in range(3):
        turn_cos, turn_sin = t_twiddle[:128], t_twiddle[128:]
        real, imag = halves[:128, 128 * c : 128 * (c + 1)], halves[128:, 128 * c : 128 * (c + 1)]
        joined.append(
            jnp.concatenate([real * turn_cos + imag * turn_sin, imag * turn_cos - real * turn_sin], axis=1)
        )
    modes = dot(jnp.concatenate(joined, axis=0), t_straight[...])
    own = iota((384, 256), 0) % 8 == iota((384, 256), 1) // 2 % 8
    pick = (iota((48, 384), 1) // 8 == iota((48, 384), 0)).astype(F32)
    modes = dot(pick, jnp.where(own, modes, 0.0))
    note = jnp.where(iota((1, LANES), 1) % 2 == 0, shift[azi].astype(F32), rest[azi])
    for h in range(2):
        for q in range(16):
            for c in range(3):
                spec_out[16 * h + q, c, :] = modes[16 * c + q, 128 * h : 128 * (h + 1)]
            spec_out[16 * h + q, 3, :] = note[0]
    every(AZI, lambda s: to_azi(2, spec_out.at[target(s)], spec_in.at[azi], s))
    later(2, spec_in.at[pl.ds(1, AZI - 1)])
    spec_in[azi] = spec_out[azi]

    for one in halos:
        one.wait_recv()

    sides = col_in[...].T
    lane_two = iota((2, LANES), 1)
    for m in range(MEMBERS):
        ext[m, pl.ds(0, SLAB), pl.ds(SEG, LANES)] = sides[SLAB * m : SLAB * (m + 1)]
    for m in range(MEMBERS):
        pair = pl.ds(2 * m, 2)
        for n, (at, edge_at, at_edge) in enumerate(
            ((EXT_R - 2, 0, rad == 0), (SLAB, SLAB - 1, rad == RAD - 1))
        ):
            edge = ext[m, pl.ds(edge_at, 1), :]
            far = jnp.where(lane_two < LANES // 2, tile_in[2 * n + 1, pair, :], tile_in[2 * n, pair, :])
            got = jnp.concatenate([row_in[n, pair, :], far], axis=1)
            ext[m, pl.ds(at, 2), :] = jnp.where(at_edge, jnp.broadcast_to(edge, (2, EXT_P)), got)

    coeffs = [wide(coef[n], EXT_P // LANES) for n in range(3)]
    for z in range(NZ):
        change, center = rates(lambda c, zz: ext[NZ * c + zz], z, EXT_R, coeffs)
        for c in range(3):
            sect[NZ * c + z] = center[c] + change[c]
    for m in range(MEMBERS):
        top = sect[m, pl.ds(0, 1), :]
        sect[m, pl.ds(EXT_R - 1, 1), :] = jnp.where(rad == 0, top, sect[m, pl.ds(EXT_R - 1, 1), :])
        low = sect[m, pl.ds(SLAB - 1, 1), :]
        sect[m, pl.ds(SLAB, 1), :] = jnp.where(rad == RAD - 1, low, sect[m, pl.ds(SLAB, 1), :])
    coeffs = [wide(coef[n, pl.ds(0, SLAB), :], EXT_P // LANES) for n in range(3)]
    weights = [weight[n] for n in range(4)]
    for z in range(NZ):
        change, center = rates(lambda c, zz: sect[NZ * c + zz], z, SLAB, coeffs)
        for c in range(3):
            m = NZ * c + z
            hydro = 0.5 * ext[m, pl.ds(0, SLAB), :] + 0.5 * (center[c] + change[c])
            ahead = pltpu.roll(hydro, EXT_P - 1, 1)
            behind = pltpu.roll(hydro, 1, 1)
            behind_two = pltpu.roll(hydro, 2, 1)
            for quad in range(QUADS):
                lanes = slice(LANES * quad, LANES * (quad + 1))
                moved = (
                    weights[0] * ahead[:, lanes] + weights[1] * hydro[:, lanes]
                    + weights[2] * behind[:, lanes] + weights[3] * behind_two[:, lanes]
                )
                for block in range(SLAB // 8):
                    move_out[pl.ds(8 * ROWS * block + MEMBERS * quad + m, 8, stride=ROWS), :] = moved[
                        8 * block : 8 * block + 8
                    ]

    every(AZI, lambda s: to_azi(1, move_out.at[rows(target(s))], cycle_in.at[rows(azi)], s))
    later(1, cycle_in.at[pl.ds(0, ROWS * (AZI - 1))])
    cycle_in[rows(azi), :] = move_out[rows(azi), :]

    wait_all(2, spec_in.at[pl.ds(1, AZI - 1)], recv_sem)
    tile_lane = iota((AZI // 2, LANES), 1) // 16
    parts = [spec_in[pl.ds(16 * h, 16), c, :] for h in range(2) for c in range(4)]
    for n in range(RAD):
        packed = parts[0] if n == 0 else pltpu.roll(parts[0], LANES - 16 * n, 1)
        for at in range(1, 8):
            turn = 16 * (at - n) % LANES
            packed = jnp.where(tile_lane == at, pltpu.roll(parts[at], turn, 1) if turn else parts[at], packed)
        modes_out[n] = packed
    every(RAD, lambda s: to_rad(4, modes_out.at[ring(s)], modes_in.at[rad], s))
    later(4, modes_in.at[pl.ds(1, RAD - 1)])
    modes_in[rad] = modes_out[rad]

    wait_all(1, cycle_in.at[pl.ds(0, ROWS * (AZI - 1))], recv_sem)
    cycle_in[pl.ds(ROWS * AZI, ROWS), :] = cycle_in[pl.ds(0, ROWS), :]
    my_shift = shift[azi]
    turn_rows, turn_lanes = my_shift // LANES, my_shift % LANES
    lane = iota((ROWS, LANES), 1)

    def rotated(segment):
        start = lax.rem(QUADS * segment + LANES - 1 - turn_rows + LANES, LANES) * MEMBERS
        here = cycle_in[pl.ds(start + MEMBERS, ROWS), :]
        before = cycle_in[pl.ds(start, ROWS), :]
        return pltpu.roll(jnp.where(lane < LANES - turn_lanes, here, before), turn_lanes, 1)

    def rotate_and_send(step, carry):
        segment = target(step)
        cycle_out[rows(segment), :] = rotated(segment)
        to_azi(3, cycle_out.at[rows(segment)], move_in.at[rows(azi)], step).start()
        return carry

    lax.fori_loop(1, AZI, rotate_and_send, 0)
    later(3, move_in.at[pl.ds(0, ROWS * (AZI - 1))])
    move_in[rows(azi), :] = rotated(azi)

    shape = (16, NR)
    mode = 256 * rad + 8 * azi + iota(shape, 0) // 2
    part = iota(shape, 0) % 2
    at_cycle = iota(shape, 1)
    theta = (2.0 * np.pi / NPHI) * mode.astype(F32)
    wave_cos, wave_sin = jnp.cos(theta), jnp.sin(theta)
    double_cos, double_sin = jnp.cos(2.0 * theta), jnp.sin(2.0 * theta)
    cycle_radius = 1.0 + 4.0 * (at_cycle.astype(F32) + 0.5) / NR
    cycle_steep = 1.0 / (cycle_radius * jnp.sqrt(cycle_radius))
    courant, coriolis, epicycle = 0.3 / cycle_radius, 0.2 * cycle_steep, 0.05 * cycle_steep
    drift = courant * wave_sin
    bend = 2.0 * wave_cos - 2.0

    def times_i(value):
        return jnp.where(part == 0, -pltpu.roll(value, 15, 0), pltpu.roll(value, 1, 0))

    def neighbours(value):
        behind = jnp.where(at_cycle == 0, value, pltpu.roll(value, 1, 1))
        ahead = jnp.where(at_cycle == NR - 1, value, pltpu.roll(value, NR - 1, 1))
        return 0.5 * (ahead - behind), (ahead + behind - 2.0 * value) + bend * value

    loads[6].wait()
    wait_all(4, modes_in.at[pl.ds(1, RAD - 1)], recv_sem)
    arrived = []
    for n in range(RAD):
        arrived += [modes_in[n], pltpu.roll(modes_in[n], LANES // 2, 1)]
    arrived = jnp.concatenate(arrived, axis=0).T
    rho, ur, up, extra = [arrived[16 * c : 16 * (c + 1)] for c in range(4)]
    cycle_turn = jnp.where(part == 0, extra, pltpu.roll(extra, 1, 0)).astype(jnp.int32)
    fraction = jnp.where(part == 0, pltpu.roll(extra, 15, 0), extra)
    phase = (2.0 * np.pi / NPHI) * ((mode * cycle_turn) & (NPHI - 1)).astype(F32)
    phase_cos, phase_sin = jnp.cos(phase), jnp.sin(phase)
    w_next, w_here, w_prev, w_prev_two = cubic_weights(fraction)
    mix_real = (w_next + w_prev) * wave_cos + w_here + w_prev_two * double_cos
    mix_imag = (w_next - w_prev) * wave_sin - w_prev_two * double_sin
    turn_real = mix_real * phase_cos + mix_imag * phase_sin
    turn_imag = mix_imag * phase_cos - mix_real * phase_sin
    rho_diff, rho_spread = neighbours(rho)
    ur_diff, ur_spread = neighbours(ur)
    rho_one = rho - (RADIAL_COURANT * ur_diff + drift * times_i(up)) + VISCOSITY * rho_spread
    ur_one = ur + coriolis * up - RADIAL_COURANT * rho_diff + VISCOSITY * ur_spread
    up_one = up - epicycle * ur - drift * times_i(rho) + VISCOSITY * neighbours(up)[1]
    change = VISCOSITY * neighbours(rho_one)[1] - (
        RADIAL_COURANT * neighbours(ur_one)[0] + drift * times_i(up_one)
    )
    surface = 0.5 * rho + 0.5 * (rho_one + change)
    spectrum = (turn_real * surface + turn_imag * times_i(surface)).astype(jnp.bfloat16)

    mode_potential = jnp.zeros(shape, F32)
    for k in range(8):
        product = lax.dot_general(
            spectrum, kern[k], (((1,), (1,)), ((), ())), preferred_element_type=F32
        )
        mode_potential = jnp.where(iota(shape, 0) // 2 == k, product, mode_potential)
    for h in range(2):
        pot_out[h] = mode_potential[:, LANES * h : LANES * (h + 1)]
    every(RAD, lambda s: to_rad(5, pot_out.at[ring(s) // 4], pot_in.at[rad], s))
    later(5, pot_in.at[pl.ds(1, RAD - 1)])
    pot_in[rad] = pot_out[rad // 4]
    wait_all(5, pot_in.at[pl.ds(1, RAD - 1)], recv_sem)
    lines[...] = pot_in[...].reshape(LANES, LANES).T
    gathered = lines[rows(lax.rem(rad, 4), SLAB), :]
    for n in range(SLAB):
        back_out[n, 0, :] = gathered[n]
    every(AZI, lambda s: to_azi(6, back_out.at[target(s)], back_in.at[azi], s))
    later(6, back_in.at[pl.ds(1, AZI - 1)])
    back_in[azi] = back_out[azi]
    for load in loads[7:9]:
        load.wait()
    wait_all(6, back_in.at[pl.ds(1, AZI - 1)], recv_sem)
    values = back_in[:, 0, :]
    values = jnp.concatenate([values[:16], values[16:]], axis=1)
    spread = (iota((128, 16), 0) // 8 == iota((128, 16), 1)).astype(F32)
    zero_mode = (iota((128, 256), 0) == 0) & (iota((128, 256), 1) < 2)
    own = iota((128, 256), 0) % 8 == iota((128, 256), 1) // 2 % 8
    values = jnp.where(own, dot(spread, values) * jnp.where(zero_mode, 1.0 / NPHI, 2.0 / NPHI), 0.0)
    pieces = dot(values, t_back[...])
    real, imag = pieces[:, :128], pieces[:, 128:]
    turn_cos, turn_sin = t_twiddle[:128], t_twiddle[128:]
    joined = jnp.concatenate([real * turn_cos - imag * turn_sin, real * turn_sin + imag * turn_cos], axis=0)
    potential[...] = dot(t_last[...], joined)

    wait_all(3, move_in.at[pl.ds(0, ROWS * (AZI - 1))], recv_sem)
    moved_out[...] = move_in[...]

    for wait in finish:
        wait()


def unpack(move_in, lines, density_out, radial_out, azimuthal_out, potential):
    for c, out in enumerate((density_out, radial_out, azimuthal_out)):
        for z in range(NZ):
            for quad in range(QUADS):
                for block in range(SLAB // 8):
                    at = 8 * ROWS * block + MEMBERS * quad + NZ * c + z
                    out[z, pl.ds(8 * block, 8), pl.ds(LANES * quad, LANES)] = move_in[
                        pl.ds(at, 8, stride=ROWS), :
                    ]
    potential[...] = lines[...]


def step(density, radial_velocity, azimuthal_velocity, cycle_shift, remainder, kernel):
    whole = pl.BlockSpec(memory_space=pltpu.VMEM)
    away = pl.BlockSpec(memory_space=pltpu.HBM)
    block = jax.ShapeDtypeStruct((NZ, SLAB, SEG), F32)
    moves = pltpu.VMEM((ROWS * AZI, LANES), F32)
    single = pltpu.VMEM((AZI, 1, LANES), F32)
    moved, lines = pl.pallas_call(
        body,
        name="disc_step",
        out_shape=[jax.ShapeDtypeStruct((ROWS * AZI, LANES), F32), jax.ShapeDtypeStruct((128, 128), F32)],
        in_specs=[away] * 11,
        out_specs=[whole] * 2,
        scratch_shapes=[
            pltpu.VMEM((MEMBERS, EXT_R, EXT_P), F32),
            pltpu.VMEM((MEMBERS, EXT_R, EXT_P), F32),
            pltpu.VMEM((3, EXT_R, LANES), F32),
            pltpu.VMEM((4, SLAB, LANES), F32),
            pltpu.VMEM((2, 2 * MEMBERS, EXT_P), F32),
            pltpu.VMEM((2, 2 * MEMBERS, SEG), F32),
            pltpu.VMEM((4, 2 * MEMBERS, LANES), F32),
            pltpu.VMEM((2, 8, MEMBERS * SLAB), F32),
            pltpu.VMEM((LANES, MEMBERS * SLAB), F32),
            moves,
            pltpu.VMEM((ROWS * (AZI + 1), LANES), F32),
            moves,
            moves,
            pltpu.VMEM((3, AZI, QUADS, LANES), F32),
            pltpu.VMEM((3, AZI, QUADS, LANES), F32),
            pltpu.VMEM((AZI, 4, LANES), F32),
            pltpu.VMEM((AZI, 4, LANES), F32),
            pltpu.VMEM((RAD, AZI // 2, LANES), F32),
            pltpu.VMEM((RAD, AZI // 2, LANES), F32),
            pltpu.VMEM((2, 16, LANES), F32),
            pltpu.VMEM((RAD, 16, LANES), F32),
            pltpu.VMEM((LANES, LANES), F32),
            single,
            single,
            pltpu.VMEM((8, NR, NR), jnp.bfloat16),
            pltpu.VMEM((256, 128), F32),
            pltpu.VMEM((128, 256), F32),
            pltpu.VMEM((256, 128), F32),
            pltpu.VMEM((256, 256), F32),
            pltpu.VMEM((256, 256), F32),
            pltpu.SMEM((SLAB,), jnp.int32),
            pltpu.SMEM((SLAB,), F32),
            pltpu.SemaphoreType.DMA((11,)),
            pltpu.SemaphoreType.DMA((8,)),
            pltpu.SemaphoreType.DMA((8,)),
            pltpu.SemaphoreType.DMA((7,)),
            pltpu.SemaphoreType.DMA((7,)),
        ],
        compiler_params=pltpu.CompilerParams(
            collective_id=0, has_side_effects=True, vmem_limit_bytes=40 * 1024 * 1024
        ),
    )(
        *[
            pltpu.with_memory_space_constraint(value, pltpu.HBM)
            for value in (
                density, radial_velocity, azimuthal_velocity, cycle_shift, remainder, kernel,
                *[jnp.asarray(table) for table in tables()],
            )
        ]
    )
    *fields, potential = pl.pallas_call(
        unpack,
        name="unpack",
        out_shape=[block, block, block, jax.ShapeDtypeStruct((128, 128), F32)],
        in_specs=[whole] * 2,
        out_specs=[whole] * 4,
        compiler_params=pltpu.CompilerParams(vmem_limit_bytes=8 * 1024 * 1024),
    )(moved, lines)
    return *fields, potential.reshape(1, NPHI)


def solution(mesh):
    field = P(None, "rad", "azi")
    both = P(("rad", "azi"), None)
    return jax.shard_map(
        step,
        mesh=mesh,
        in_specs=(field, field, field, P("rad"), P("rad"), P(("rad", "azi"), None, None)),
        out_specs=(field, field, field, both),
        check_vma=False,
    )
```

```python
import numpy as np

import jax
import jax.numpy as jnp
from jax import lax
from jax.experimental import pallas as pl
from jax.experimental.pallas import tpu as pltpu
from jax.sharding import PartitionSpec as P

NZ = 4
NPHI = 16384
MODES = 2048
NR = 256
RAD = 8
AZI = 32
SLAB = NR // RAD
SEG = NPHI // AZI
LANES = 128
QUADS = SEG // LANES
MEMBERS = 3 * NZ
WORDS = MEMBERS // 2
ROWS = WORDS * QUADS
CODES = 32767
OCTAVES = 28.0
TOP = 4.0
EXT_R = SLAB + 8
EXT_P = SEG + LANES
RADIAL_COURANT = 0.3
VISCOSITY = 0.08
HIGHEST = lax.Precision.HIGHEST
F32 = jnp.float32
MESH = pl.DeviceIdType.MESH


def tables():
    n = np.arange(128)
    turn = 2.0 * np.pi / 128 * (np.outer(n, n) % 128)
    first = np.concatenate([np.cos(turn), -np.sin(turn)], axis=0)
    last = np.concatenate([np.cos(turn), -np.sin(turn)], axis=1)
    small = 2.0 * np.pi / NPHI * np.outer(n, n)
    twiddle = np.concatenate([np.cos(small), np.sin(small)], axis=0)
    col = np.arange(256)
    half, ring, part = col // 128, col % 128 // 16, col % 2
    phi = 2.0 * np.pi / 128 * (np.outer(n, 2 * ring + half) % 128)
    cos, sin = np.cos(phi), np.sin(phi)
    real = part == 0
    straight = np.concatenate([np.where(real, cos, -sin), np.where(real, sin, cos)], axis=0)
    real = real[:, None]
    back = np.concatenate(
        [np.where(real, cos.T, -sin.T), np.where(real, sin.T, cos.T)], axis=1
    )
    return [t.astype(np.float32) for t in (first, last, twiddle, straight, back)]


def dot(left, right):
    return jnp.dot(left, right, precision=HIGHEST, preferred_element_type=F32)


def iota(shape, axis):
    return lax.broadcasted_iota(jnp.int32, shape, axis)


def wide(value, count):
    return jnp.concatenate([value] * count, axis=1)


def cubic_weights(remainder):
    moved = -remainder
    w_next = moved * (moved + 1.0) * (moved + 2.0) / 6.0
    w_here = -(moved - 1.0) * (moved + 1.0) * (moved + 2.0) / 2.0
    w_prev = (moved - 1.0) * moved * (moved + 2.0) / 2.0
    w_prev_two = -(moved - 1.0) * moved * (moved + 1.0) / 6.0
    return w_next, w_here, w_prev, w_prev_two


def encode(value):
    level = (jnp.log(jnp.abs(value)) * (1.0 / np.log(2.0)) - TOP) * (CODES / OCTAVES) + (CODES + 0.5)
    code = jnp.clip(level, 0.0, CODES + 0.5).astype(jnp.int32)
    return jnp.where(value < 0, -code, code)


def decode(code):
    level = (jnp.abs(code) - CODES).astype(F32) * (OCTAVES / CODES) + TOP
    size = jnp.where(code == 0, 0.0, jnp.exp(level * np.log(2.0)))
    return jnp.where(code < 0, -size, size)


def rates(get, z, rows, coeffs):
    courant, coriolis, epicycle = coeffs
    below, above = max(z - 1, 0), min(z + 1, NZ - 1)
    center, ahead, rad_diff, azi_diff, spread = [], [], [], [], []
    for c in range(3):
        whole = get(c, z)
        inner = pltpu.roll(whole, 1, 0)[:rows]
        outer = pltpu.roll(whole, EXT_R - 1, 0)[:rows]
        mid = whole[:rows]
        prev = pltpu.roll(mid, 1, 1)
        following = pltpu.roll(mid, EXT_P - 1, 1)
        center.append(mid)
        rad_diff.append(outer - inner if c < 2 else None)
        azi_diff.append(following - prev if c != 1 else None)
        total = (get(c, below)[:rows] + get(c, above)[:rows]) + (inner + outer) + (prev + following)
        spread.append(VISCOSITY * (total - 6.0 * mid))
    half = 0.5 * RADIAL_COURANT
    change = (
        spread[0] - (half * rad_diff[1] + courant * azi_diff[2]),
        spread[1] + coriolis * center[2] - half * rad_diff[0],
        spread[2] - epicycle * center[1] - courant * azi_diff[0],
    )
    return change, center


def body(
    density, radial_velocity, azimuthal_velocity, shift_far, rest_far, kernel, first, last, twiddle, straight,
    back, moved_out, potential,
    ext, sect, coef, weight, row_send, row_in, tile_in, col_send, col_in, move_out, cycle_in, cycle_out,
    move_in, surf_out, surf_in, spec_out, spec_in, modes_out, modes_in, pot_out, pot_in, lines, back_out,
    back_in, kern, t_first, t_last, t_twiddle, t_straight, t_back,
    shift, rest, local_sem, halo_send, halo_recv, send_sem, recv_sem,
):
    rad, azi = lax.axis_index("rad"), lax.axis_index("azi")
    outer, inner = lax.rem(rad + 1, RAD), lax.rem(rad + RAD - 1, RAD)
    right, left = lax.rem(azi + 1, AZI), lax.rem(azi + AZI - 1, AZI)

    loads = [
        pltpu.make_async_copy(src, ext.at[pl.ds(NZ * c, NZ), pl.ds(0, SLAB), pl.ds(0, SEG)], local_sem.at[c])
        for c, src in enumerate((density, radial_velocity, azimuthal_velocity))
    ]
    for n, (src, dst) in enumerate(
        (
            (first, t_first), (twiddle, t_twiddle), (straight, t_straight),
            (kernel, kern), (back, t_back), (last, t_last), (shift_far, shift), (rest_far, rest),
        )
    ):
        loads.append(pltpu.make_async_copy(src, dst, local_sem.at[3 + n]))
    for load in loads:
        load.start()

    col_in[...] = jnp.zeros(col_in.shape, F32)
    barrier = pltpu.get_barrier_semaphore()

    def greet_azi(step, carry):
        pl.semaphore_signal(
            barrier, inc=1, device_id={"rad": rad, "azi": lax.rem(azi + step, AZI)}, device_id_type=MESH
        )
        return carry

    def greet_rad(step, carry):
        pl.semaphore_signal(
            barrier, inc=1, device_id={"rad": lax.rem(rad + step, RAD), "azi": azi}, device_id_type=MESH
        )
        return carry

    for r_to in (outer, inner):
        for a_to in (right, left):
            pl.semaphore_signal(barrier, inc=1, device_id={"rad": r_to, "azi": a_to}, device_id_type=MESH)
    lax.fori_loop(1, AZI, greet_azi, 0)
    lax.fori_loop(1, RAD, greet_rad, 0)

    row = iota((EXT_R, LANES), 0)
    cycle = SLAB * rad + jnp.where(row < SLAB + 4, row, row - EXT_R)
    radius = 1.0 + 4.0 * (cycle.astype(F32) + 0.5) / NR
    steep = 1.0 / (radius * jnp.sqrt(radius))
    coef[0] = 0.15 / radius
    coef[1] = 0.2 * steep
    coef[2] = 0.05 * steep
    for load in loads[9:]:
        load.wait()
    block_row = iota((8, LANES), 0)
    for block in range(SLAB // 8):
        fraction = jnp.zeros((8, LANES), F32)
        for n in range(8):
            fraction = jnp.where(block_row == n, rest[8 * block + n], fraction)
        for n, value in enumerate(cubic_weights(fraction)):
            weight[n, pl.ds(8 * block, 8), :] = value
    ext[:, pl.ds(SLAB, 8), :] = jnp.zeros((MEMBERS, 8, EXT_P), F32)

    for load in loads[:3]:
        load.wait()
    lane_tile = iota((SLAB, LANES), 1)
    mixed = []
    for m in range(MEMBERS):
        low = ext[m, pl.ds(0, SLAB), pl.ds(0, LANES)]
        high = ext[m, pl.ds(0, SLAB), pl.ds(SEG - LANES, LANES)]
        edge = jnp.where(lane_tile < LANES // 2, low, high)
        mixed.append(edge)
        for n, at in enumerate((SLAB - 2, 0)):
            row_send[n, pl.ds(2 * m, 2), pl.ds(0, SEG)] = ext[m, pl.ds(at, 2), pl.ds(0, SEG)]
            row_send[n, pl.ds(2 * m, 2), pl.ds(SEG, LANES)] = edge[at : at + 2]
    columns = jnp.concatenate(mixed, axis=0).T
    col_send[0] = columns[LANES - 8 :]
    col_send[1] = columns[:8]

    for c in range(3):
        heights = [ext[NZ * c + z, pl.ds(0, SLAB), pl.ds(0, SEG)] for z in range(NZ)]
        total = (heights[0] + heights[1]) + (heights[2] + heights[3])
        for n in range(SLAB):
            for quad in range(QUADS):
                surf_out[c, n, quad, :] = total[n, LANES * quad : LANES * (quad + 1)]

    pl.semaphore_wait(barrier, AZI - 1 + RAD - 1 + 4)

    def halo(n, src, dst, r_to, a_to):
        return pltpu.make_async_remote_copy(
            src_ref=src, dst_ref=dst, send_sem=halo_send.at[n], recv_sem=halo_recv.at[n],
            device_id={"rad": r_to, "azi": a_to}, device_id_type=MESH,
        )

    plain, corner = pl.ds(0, SEG), pl.ds(SEG, LANES)
    halos = [
        halo(0, row_send.at[0, :, plain], row_in.at[0], outer, azi),
        halo(1, row_send.at[1, :, plain], row_in.at[1], inner, azi),
        halo(2, col_send.at[0], col_in.at[pl.ds(LANES - 8, 8)], rad, right),
        halo(3, col_send.at[1], col_in.at[pl.ds(0, 8)], rad, left),
        halo(4, row_send.at[0, :, corner], tile_in.at[0], outer, right),
        halo(5, row_send.at[0, :, corner], tile_in.at[1], outer, left),
        halo(6, row_send.at[1, :, corner], tile_in.at[2], inner, right),
        halo(7, row_send.at[1, :, corner], tile_in.at[3], inner, left),
    ]
    for one in halos:
        one.start()
    finish = [one.wait_send for one in halos]
    def to_azi(n, src, dst, step):
        return pltpu.make_async_remote_copy(
            src_ref=src, dst_ref=dst, send_sem=send_sem.at[n], recv_sem=recv_sem.at[n],
            device_id={"rad": rad, "azi": lax.rem(azi + step, AZI)}, device_id_type=MESH,
        )

    def to_rad(n, src, dst, step):
        return pltpu.make_async_remote_copy(
            src_ref=src, dst_ref=dst, send_sem=send_sem.at[n], recv_sem=recv_sem.at[n],
            device_id={"rad": lax.rem(rad + step, RAD), "azi": azi}, device_id_type=MESH,
        )

    def every(count, make):
        def one(step, carry):
            make(step).start()
            return carry

        lax.fori_loop(1, count, one, 0)

    def rows(index, size=ROWS):
        return pl.ds(pl.multiple_of(index * size, 8), size)

    def wait_all(n, ref, sem):
        pltpu.make_async_copy(ref, ref, sem.at[n]).wait()

    def later(n, ref):
        finish.append(lambda: wait_all(n, ref, send_sem))

    def target(step):
        return lax.rem(azi + step, AZI)

    def ring(step):
        return lax.rem(rad + step, RAD)

    every(AZI, lambda s: to_azi(0, surf_out.at[:, target(s)], surf_in.at[:, azi], s))
    later(0, surf_in.at[:, pl.ds(1, AZI - 1)])
    for c in range(3):
        surf_in[c, azi] = surf_out[c, azi]

    for load in loads[3:6]:
        load.wait()
    wait_all(0, surf_in.at[:, pl.ds(1, AZI - 1)], recv_sem)
    sums = jnp.concatenate([surf_in[c].reshape(128, 128) for c in range(3)], axis=1)
    halves = dot(t_first[...], sums)
    joined = []
    for c in range(3):
        turn_cos, turn_sin = t_twiddle[:128], t_twiddle[128:]
        real, imag = halves[:128, 128 * c : 128 * (c + 1)], halves[128:, 128 * c : 128 * (c + 1)]
        joined.append(
            jnp.concatenate([real * turn_cos + imag * turn_sin, imag * turn_cos - real * turn_sin], axis=1)
        )
    modes = dot(jnp.concatenate(joined, axis=0), t_straight[...])
    own = iota((384, 256), 0) % 8 == iota((384, 256), 1) // 2 % 8
    pick = (iota((48, 384), 1) // 8 == iota((48, 384), 0)).astype(F32)
    modes = dot(pick, jnp.where(own, modes, 0.0))
    note = jnp.where(iota((1, LANES), 1) % 2 == 0, shift[azi].astype(F32), rest[azi])
    for h in range(2):
        for q in range(16):
            for c in range(3):
                spec_out[16 * h + q, c, :] = modes[16 * c + q, 128 * h : 128 * (h + 1)]
            spec_out[16 * h + q, 3, :] = note[0]
    every(AZI, lambda s: to_azi(2, spec_out.at[target(s)], spec_in.at[azi], s))
    later(2, spec_in.at[pl.ds(1, AZI - 1)])
    spec_in[azi] = spec_out[azi]

    for one in halos:
        one.wait_recv()

    sides = col_in[...].T
    lane_two = iota((2, LANES), 1)
    for m in range(MEMBERS):
        ext[m, pl.ds(0, SLAB), pl.ds(SEG, LANES)] = sides[SLAB * m : SLAB * (m + 1)]
    for m in range(MEMBERS):
        pair = pl.ds(2 * m, 2)
        for n, (at, edge_at, at_edge) in enumerate(
            ((EXT_R - 2, 0, rad == 0), (SLAB, SLAB - 1, rad == RAD - 1))
        ):
            edge = ext[m, pl.ds(edge_at, 1), :]
            far = jnp.where(lane_two < LANES // 2, tile_in[2 * n + 1, pair, :], tile_in[2 * n, pair, :])
            got = jnp.concatenate([row_in[n, pair, :], far], axis=1)
            ext[m, pl.ds(at, 2), :] = jnp.where(at_edge, jnp.broadcast_to(edge, (2, EXT_P)), got)

    coeffs = [wide(coef[n], EXT_P // LANES) for n in range(3)]
    for z in range(NZ):
        change, center = rates(lambda c, zz: ext[NZ * c + zz], z, EXT_R, coeffs)
        for c in range(3):
            sect[NZ * c + z] = center[c] + change[c]
    for m in range(MEMBERS):
        top = sect[m, pl.ds(0, 1), :]
        sect[m, pl.ds(EXT_R - 1, 1), :] = jnp.where(rad == 0, top, sect[m, pl.ds(EXT_R - 1, 1), :])
        low = sect[m, pl.ds(SLAB - 1, 1), :]
        sect[m, pl.ds(SLAB, 1), :] = jnp.where(rad == RAD - 1, low, sect[m, pl.ds(SLAB, 1), :])
    coeffs = [wide(coef[n, pl.ds(0, SLAB), :], EXT_P // LANES) for n in range(3)]
    weights = [weight[n] for n in range(4)]
    lower = {}
    for z in range(NZ):
        change, center = rates(lambda c, zz: sect[NZ * c + zz], z, SLAB, coeffs)
        for c in range(3):
            m = NZ * c + z
            hydro = 0.5 * ext[m, pl.ds(0, SLAB), :] + 0.5 * (center[c] + change[c])
            ahead = pltpu.roll(hydro, EXT_P - 1, 1)
            behind = pltpu.roll(hydro, 1, 1)
            behind_two = pltpu.roll(hydro, 2, 1)
            for quad in range(QUADS):
                lanes = slice(LANES * quad, LANES * (quad + 1))
                moved = (
                    weights[0] * ahead[:, lanes] + weights[1] * hydro[:, lanes]
                    + weights[2] * behind[:, lanes] + weights[3] * behind_two[:, lanes]
                )
                code = encode(moved)
                if z % 2 == 0:
                    lower[c, quad] = code & 0xFFFF
                    continue
                words = (code << 16) | lower[c, quad]
                for block in range(SLAB // 8):
                    at = 8 * ROWS * block + WORDS * quad + 2 * c + z // 2
                    move_out[pl.ds(at, 8, stride=ROWS), :] = words[8 * block : 8 * block + 8]

    every(AZI, lambda s: to_azi(1, move_out.at[rows(target(s))], cycle_in.at[rows(azi)], s))
    later(1, cycle_in.at[pl.ds(0, ROWS * (AZI - 1))])
    cycle_in[rows(azi), :] = move_out[rows(azi), :]

    wait_all(2, spec_in.at[pl.ds(1, AZI - 1)], recv_sem)
    tile_lane = iota((AZI // 2, LANES), 1) // 16
    parts = [spec_in[pl.ds(16 * h, 16), c, :] for h in range(2) for c in range(4)]
    for n in range(RAD):
        packed = parts[0] if n == 0 else pltpu.roll(parts[0], LANES - 16 * n, 1)
        for at in range(1, 8):
            turn = 16 * (at - n) % LANES
            packed = jnp.where(tile_lane == at, pltpu.roll(parts[at], turn, 1) if turn else parts[at], packed)
        modes_out[n] = packed
    every(RAD, lambda s: to_rad(4, modes_out.at[ring(s)], modes_in.at[rad], s))
    later(4, modes_in.at[pl.ds(1, RAD - 1)])
    modes_in[rad] = modes_out[rad]

    wait_all(1, cycle_in.at[pl.ds(0, ROWS * (AZI - 1))], recv_sem)
    cycle_in[pl.ds(ROWS * AZI, ROWS), :] = cycle_in[pl.ds(0, ROWS), :]
    my_shift = shift[azi]
    turn_rows, turn_lanes = my_shift // LANES, my_shift % LANES
    lane = iota((ROWS, LANES), 1)

    def rotated(segment):
        start = lax.rem(QUADS * segment + LANES - 1 - turn_rows + LANES, LANES) * WORDS
        here = cycle_in[pl.ds(start + WORDS, ROWS), :]
        before = cycle_in[pl.ds(start, ROWS), :]
        return pltpu.roll(jnp.where(lane < LANES - turn_lanes, here, before), turn_lanes, 1)

    def rotate_and_send(step, carry):
        segment = target(step)
        cycle_out[rows(segment), :] = rotated(segment)
        to_azi(3, cycle_out.at[rows(segment)], move_in.at[rows(azi)], step).start()
        return carry

    lax.fori_loop(1, AZI, rotate_and_send, 0)
    later(3, move_in.at[pl.ds(0, ROWS * (AZI - 1))])
    move_in[rows(azi), :] = rotated(azi)

    shape = (16, NR)
    mode = 256 * rad + 8 * azi + iota(shape, 0) // 2
    part = iota(shape, 0) % 2
    at_cycle = iota(shape, 1)
    theta = (2.0 * np.pi / NPHI) * mode.astype(F32)
    wave_cos, wave_sin = jnp.cos(theta), jnp.sin(theta)
    double_cos, double_sin = jnp.cos(2.0 * theta), jnp.sin(2.0 * theta)
    cycle_radius = 1.0 + 4.0 * (at_cycle.astype(F32) + 0.5) / NR
    cycle_steep = 1.0 / (cycle_radius * jnp.sqrt(cycle_radius))
    courant, coriolis, epicycle = 0.3 / cycle_radius, 0.2 * cycle_steep, 0.05 * cycle_steep
    drift = courant * wave_sin
    bend = 2.0 * wave_cos - 2.0

    def times_i(value):
        return jnp.where(part == 0, -pltpu.roll(value, 15, 0), pltpu.roll(value, 1, 0))

    def neighbours(value):
        behind = jnp.where(at_cycle == 0, value, pltpu.roll(value, 1, 1))
        ahead = jnp.where(at_cycle == NR - 1, value, pltpu.roll(value, NR - 1, 1))
        return 0.5 * (ahead - behind), (ahead + behind - 2.0 * value) + bend * value

    loads[6].wait()
    wait_all(4, modes_in.at[pl.ds(1, RAD - 1)], recv_sem)
    arrived = []
    for n in range(RAD):
        arrived += [modes_in[n], pltpu.roll(modes_in[n], LANES // 2, 1)]
    arrived = jnp.concatenate(arrived, axis=0).T
    rho, ur, up, extra = [arrived[16 * c : 16 * (c + 1)] for c in range(4)]
    cycle_turn = jnp.where(part == 0, extra, pltpu.roll(extra, 1, 0)).astype(jnp.int32)
    fraction = jnp.where(part == 0, pltpu.roll(extra, 15, 0), extra)
    phase = (2.0 * np.pi / NPHI) * ((mode * cycle_turn) & (NPHI - 1)).astype(F32)
    phase_cos, phase_sin = jnp.cos(phase), jnp.sin(phase)
    w_next, w_here, w_prev, w_prev_two = cubic_weights(fraction)
    mix_real = (w_next + w_prev) * wave_cos + w_here + w_prev_two * double_cos
    mix_imag = (w_next - w_prev) * wave_sin - w_prev_two * double_sin
    turn_real = mix_real * phase_cos + mix_imag * phase_sin
    turn_imag = mix_imag * phase_cos - mix_real * phase_sin
    rho_diff, rho_spread = neighbours(rho)
    ur_diff, ur_spread = neighbours(ur)
    rho_one = rho - (RADIAL_COURANT * ur_diff + drift * times_i(up)) + VISCOSITY * rho_spread
    ur_one = ur + coriolis * up - RADIAL_COURANT * rho_diff + VISCOSITY * ur_spread
    up_one = up - epicycle * ur - drift * times_i(rho) + VISCOSITY * neighbours(up)[1]
    change = VISCOSITY * neighbours(rho_one)[1] - (
        RADIAL_COURANT * neighbours(ur_one)[0] + drift * times_i(up_one)
    )
    surface = 0.5 * rho + 0.5 * (rho_one + change)
    spectrum = (turn_real * surface + turn_imag * times_i(surface)).astype(jnp.bfloat16)

    mode_potential = jnp.zeros(shape, F32)
    for k in range(8):
        product = lax.dot_general(
            spectrum, kern[k], (((1,), (1,)), ((), ())), preferred_element_type=F32
        )
        mode_potential = jnp.where(iota(shape, 0) // 2 == k, product, mode_potential)
    for h in range(2):
        pot_out[h] = mode_potential[:, LANES * h : LANES * (h + 1)]
    every(RAD, lambda s: to_rad(5, pot_out.at[ring(s) // 4], pot_in.at[rad], s))
    later(5, pot_in.at[pl.ds(1, RAD - 1)])
    pot_in[rad] = pot_out[rad // 4]
    wait_all(5, pot_in.at[pl.ds(1, RAD - 1)], recv_sem)
    lines[...] = pot_in[...].reshape(LANES, LANES).T
    gathered = lines[rows(lax.rem(rad, 4), SLAB), :]
    for n in range(SLAB):
        back_out[n, 0, :] = gathered[n]
    every(AZI, lambda s: to_azi(6, back_out.at[target(s)], back_in.at[azi], s))
    later(6, back_in.at[pl.ds(1, AZI - 1)])
    back_in[azi] = back_out[azi]
    for load in loads[7:9]:
        load.wait()
    wait_all(6, back_in.at[pl.ds(1, AZI - 1)], recv_sem)
    values = back_in[:, 0, :]
    values = jnp.concatenate([values[:16], values[16:]], axis=1)
    spread = (iota((128, 16), 0) // 8 == iota((128, 16), 1)).astype(F32)
    zero_mode = (iota((128, 256), 0) == 0) & (iota((128, 256), 1) < 2)
    own = iota((128, 256), 0) % 8 == iota((128, 256), 1) // 2 % 8
    values = jnp.where(own, dot(spread, values) * jnp.where(zero_mode, 1.0 / NPHI, 2.0 / NPHI), 0.0)
    pieces = dot(values, t_back[...])
    real, imag = pieces[:, :128], pieces[:, 128:]
    turn_cos, turn_sin = t_twiddle[:128], t_twiddle[128:]
    joined = jnp.concatenate([real * turn_cos - imag * turn_sin, real * turn_sin + imag * turn_cos], axis=0)
    potential[...] = dot(t_last[...], joined)

    wait_all(3, move_in.at[pl.ds(0, ROWS * (AZI - 1))], recv_sem)
    moved_out[...] = move_in[...]

    for wait in finish:
        wait()


def unpack(move_in, lines, density_out, radial_out, azimuthal_out, potential):
    for c, out in enumerate((density_out, radial_out, azimuthal_out)):
        for pair in range(NZ // 2):
            for quad in range(QUADS):
                for block in range(SLAB // 8):
                    at = 8 * ROWS * block + WORDS * quad + 2 * c + pair
                    words = move_in[pl.ds(at, 8, stride=ROWS), :]
                    place = pl.ds(8 * block, 8), pl.ds(LANES * quad, LANES)
                    out[2 * pair, *place] = decode((words << 16) >> 16)
                    out[2 * pair + 1, *place] = decode(words >> 16)
    potential[...] = lines[...]


def step(density, radial_velocity, azimuthal_velocity, cycle_shift, remainder, kernel):
    whole = pl.BlockSpec(memory_space=pltpu.VMEM)
    away = pl.BlockSpec(memory_space=pltpu.HBM)
    block = jax.ShapeDtypeStruct((NZ, SLAB, SEG), F32)
    moves = pltpu.VMEM((ROWS * AZI, LANES), jnp.int32)
    single = pltpu.VMEM((AZI, 1, LANES), F32)
    moved, lines = pl.pallas_call(
        body,
        name="disc_step",
        out_shape=[jax.ShapeDtypeStruct((ROWS * AZI, LANES), jnp.int32), jax.ShapeDtypeStruct((128, 128), F32)],
        in_specs=[away] * 11,
        out_specs=[whole] * 2,
        scratch_shapes=[
            pltpu.VMEM((MEMBERS, EXT_R, EXT_P), F32),
            pltpu.VMEM((MEMBERS, EXT_R, EXT_P), F32),
            pltpu.VMEM((3, EXT_R, LANES), F32),
            pltpu.VMEM((4, SLAB, LANES), F32),
            pltpu.VMEM((2, 2 * MEMBERS, EXT_P), F32),
            pltpu.VMEM((2, 2 * MEMBERS, SEG), F32),
            pltpu.VMEM((4, 2 * MEMBERS, LANES), F32),
            pltpu.VMEM((2, 8, MEMBERS * SLAB), F32),
            pltpu.VMEM((LANES, MEMBERS * SLAB), F32),
            moves,
            pltpu.VMEM((ROWS * (AZI + 1), LANES), jnp.int32),
            moves,
            moves,
            pltpu.VMEM((3, AZI, QUADS, LANES), F32),
            pltpu.VMEM((3, AZI, QUADS, LANES), F32),
            pltpu.VMEM((AZI, 4, LANES), F32),
            pltpu.VMEM((AZI, 4, LANES), F32),
            pltpu.VMEM((RAD, AZI // 2, LANES), F32),
            pltpu.VMEM((RAD, AZI // 2, LANES), F32),
            pltpu.VMEM((2, 16, LANES), F32),
            pltpu.VMEM((RAD, 16, LANES), F32),
            pltpu.VMEM((LANES, LANES), F32),
            single,
            single,
            pltpu.VMEM((8, NR, NR), jnp.bfloat16),
            pltpu.VMEM((256, 128), F32),
            pltpu.VMEM((128, 256), F32),
            pltpu.VMEM((256, 128), F32),
            pltpu.VMEM((256, 256), F32),
            pltpu.VMEM((256, 256), F32),
            pltpu.SMEM((SLAB,), jnp.int32),
            pltpu.SMEM((SLAB,), F32),
            pltpu.SemaphoreType.DMA((11,)),
            pltpu.SemaphoreType.DMA((8,)),
            pltpu.SemaphoreType.DMA((8,)),
            pltpu.SemaphoreType.DMA((7,)),
            pltpu.SemaphoreType.DMA((7,)),
        ],
        compiler_params=pltpu.CompilerParams(
            collective_id=0, has_side_effects=True, vmem_limit_bytes=40 * 1024 * 1024
        ),
    )(
        *[
            pltpu.with_memory_space_constraint(value, pltpu.HBM)
            for value in (
                density, radial_velocity, azimuthal_velocity, cycle_shift, remainder, kernel,
                *[jnp.asarray(table) for table in tables()],
            )
        ]
    )
    *fields, potential = pl.pallas_call(
        unpack,
        name="unpack",
        out_shape=[block, block, block, jax.ShapeDtypeStruct((128, 128), F32)],
        in_specs=[whole] * 2,
        out_specs=[whole] * 4,
        compiler_params=pltpu.CompilerParams(vmem_limit_bytes=8 * 1024 * 1024),
    )(moved, lines)
    return *fields, potential.reshape(1, NPHI)


def solution(mesh):
    field = P(None, "rad", "azi")
    both = P(("rad", "azi"), None)
    return jax.shard_map(
        step,
        mesh=mesh,
        in_specs=(field, field, field, P("rad"), P("rad"), P(("rad", "azi"), None, None)),
        out_specs=(field, field, field, both),
        check_vma=False,
    )
```

```python
import numpy as np

import jax
import jax.numpy as jnp
from jax import lax
from jax.experimental import pallas as pl
from jax.experimental.pallas import tpu as pltpu
from jax.sharding import PartitionSpec as P

NZ = 4
NPHI = 16384
MODES = 2048
NR = 256
RAD = 8
AZI = 32
SLAB = NR // RAD
SEG = NPHI // AZI
LANES = 128
QUADS = SEG // LANES
MEMBERS = 3 * NZ
WORDS = MEMBERS // 2
ROWS = WORDS * QUADS
FIRST_MOVES = 9
CODES = 32767
OCTAVES = 28.0
TOP = 4.0
EXT_R = SLAB + 8
EXT_P = SEG + LANES
RADIAL_COURANT = 0.3
VISCOSITY = 0.08
HIGHEST = lax.Precision.HIGHEST
F32 = jnp.float32
MESH = pl.DeviceIdType.MESH


def tables():
    n = np.arange(128)
    turn = 2.0 * np.pi / 128 * (np.outer(n, n) % 128)
    first = np.concatenate([np.cos(turn), -np.sin(turn)], axis=0)
    last = np.concatenate([np.cos(turn), -np.sin(turn)], axis=1)
    small = 2.0 * np.pi / NPHI * np.outer(n, n)
    twiddle = np.concatenate([np.cos(small), np.sin(small)], axis=0)
    col = np.arange(256)
    half, ring, part = col // 128, col % 128 // 16, col % 2
    phi = 2.0 * np.pi / 128 * (np.outer(n, 2 * ring + half) % 128)
    cos, sin = np.cos(phi), np.sin(phi)
    real = part == 0
    straight = np.concatenate([np.where(real, cos, -sin), np.where(real, sin, cos)], axis=0)
    real = real[:, None]
    back = np.concatenate(
        [np.where(real, cos.T, -sin.T), np.where(real, sin.T, cos.T)], axis=1
    )
    return [t.astype(np.float32) for t in (first, last, twiddle, straight, back)]


def dot(left, right):
    return jnp.dot(left, right, precision=HIGHEST, preferred_element_type=F32)


def iota(shape, axis):
    return lax.broadcasted_iota(jnp.int32, shape, axis)


def wide(value, count):
    return jnp.concatenate([value] * count, axis=1)


def cubic_weights(remainder):
    moved = -remainder
    w_next = moved * (moved + 1.0) * (moved + 2.0) / 6.0
    w_here = -(moved - 1.0) * (moved + 1.0) * (moved + 2.0) / 2.0
    w_prev = (moved - 1.0) * moved * (moved + 2.0) / 2.0
    w_prev_two = -(moved - 1.0) * moved * (moved + 1.0) / 6.0
    return w_next, w_here, w_prev, w_prev_two


def encode(value):
    level = (jnp.log(jnp.abs(value)) * (1.0 / np.log(2.0)) - TOP) * (CODES / OCTAVES) + (CODES + 0.5)
    code = jnp.clip(level, 0.0, CODES + 0.5).astype(jnp.int32)
    return jnp.where(value < 0, -code, code)


def decode(code):
    level = (jnp.abs(code) - CODES).astype(F32) * (OCTAVES / CODES) + TOP
    size = jnp.where(code == 0, 0.0, jnp.exp(level * np.log(2.0)))
    return jnp.where(code < 0, -size, size)


def rates(get, z, rows, coeffs):
    courant, coriolis, epicycle = coeffs
    below, above = max(z - 1, 0), min(z + 1, NZ - 1)
    center, ahead, rad_diff, azi_diff, spread = [], [], [], [], []
    for c in range(3):
        whole = get(c, z)
        inner = pltpu.roll(whole, 1, 0)[:rows]
        outer = pltpu.roll(whole, EXT_R - 1, 0)[:rows]
        mid = whole[:rows]
        prev = pltpu.roll(mid, 1, 1)
        following = pltpu.roll(mid, EXT_P - 1, 1)
        center.append(mid)
        rad_diff.append(outer - inner if c < 2 else None)
        azi_diff.append(following - prev if c != 1 else None)
        total = (get(c, below)[:rows] + get(c, above)[:rows]) + (inner + outer) + (prev + following)
        spread.append(VISCOSITY * (total - 6.0 * mid))
    half = 0.5 * RADIAL_COURANT
    change = (
        spread[0] - (half * rad_diff[1] + courant * azi_diff[2]),
        spread[1] + coriolis * center[2] - half * rad_diff[0],
        spread[2] - epicycle * center[1] - courant * azi_diff[0],
    )
    return change, center


def body(
    density, radial_velocity, azimuthal_velocity, shift_far, rest_far, kernel, first, last, twiddle, straight,
    back, density_out, radial_out, azimuthal_out, potential,
    ext, sect, coef, weight, row_send, row_in, tile_in, col_send, col_in, move_out, cycle_in, cycle_out,
    move_in, surf_out, surf_in, spec_out, spec_in, modes_out, modes_in, pot_out, pot_in, lines, back_out,
    back_in, kern, t_first, t_last, t_twiddle, t_straight, t_back,
    shift, rest, local_sem, halo_send, halo_recv, send_sem, recv_sem,
):
    rad, azi = lax.axis_index("rad"), lax.axis_index("azi")
    outer, inner = lax.rem(rad + 1, RAD), lax.rem(rad + RAD - 1, RAD)
    right, left = lax.rem(azi + 1, AZI), lax.rem(azi + AZI - 1, AZI)

    loads = [
        pltpu.make_async_copy(src, ext.at[pl.ds(NZ * c, NZ), pl.ds(0, SLAB), pl.ds(0, SEG)], local_sem.at[c])
        for c, src in enumerate((density, radial_velocity, azimuthal_velocity))
    ]
    for n, (src, dst) in enumerate(
        (
            (first, t_first), (twiddle, t_twiddle), (straight, t_straight),
            (kernel, kern), (back, t_back), (last, t_last), (shift_far, shift), (rest_far, rest),
        )
    ):
        loads.append(pltpu.make_async_copy(src, dst, local_sem.at[3 + n]))
    for load in loads:
        load.start()

    col_in[...] = jnp.zeros(col_in.shape, F32)
    barrier = pltpu.get_barrier_semaphore()

    def greet_azi(step, carry):
        pl.semaphore_signal(
            barrier, inc=1, device_id={"rad": rad, "azi": lax.rem(azi + step, AZI)}, device_id_type=MESH
        )
        return carry

    def greet_rad(step, carry):
        pl.semaphore_signal(
            barrier, inc=1, device_id={"rad": lax.rem(rad + step, RAD), "azi": azi}, device_id_type=MESH
        )
        return carry

    for r_to in (outer, inner):
        for a_to in (right, left):
            pl.semaphore_signal(barrier, inc=1, device_id={"rad": r_to, "azi": a_to}, device_id_type=MESH)
    lax.fori_loop(1, AZI, greet_azi, 0)
    lax.fori_loop(1, RAD, greet_rad, 0)

    row = iota((EXT_R, LANES), 0)
    cycle = SLAB * rad + jnp.where(row < SLAB + 4, row, row - EXT_R)
    radius = 1.0 + 4.0 * (cycle.astype(F32) + 0.5) / NR
    steep = 1.0 / (radius * jnp.sqrt(radius))
    coef[0] = 0.15 / radius
    coef[1] = 0.2 * steep
    coef[2] = 0.05 * steep
    for load in loads[9:]:
        load.wait()
    block_row = iota((8, LANES), 0)
    for block in range(SLAB // 8):
        fraction = jnp.zeros((8, LANES), F32)
        for n in range(8):
            fraction = jnp.where(block_row == n, rest[8 * block + n], fraction)
        for n, value in enumerate(cubic_weights(fraction)):
            weight[n, pl.ds(8 * block, 8), :] = value
    ext[:, pl.ds(SLAB, 8), :] = jnp.zeros((MEMBERS, 8, EXT_P), F32)

    for load in loads[:3]:
        load.wait()
    for c in range(3):
        heights = [ext[NZ * c + z, pl.ds(0, SLAB), pl.ds(0, SEG)] for z in range(NZ)]
        total = (heights[0] + heights[1]) + (heights[2] + heights[3])
        for n in range(SLAB):
            for quad in range(QUADS):
                surf_out[c, n, quad, :] = total[n, LANES * quad : LANES * (quad + 1)]

    lane_tile = iota((SLAB, LANES), 1)
    mixed = []
    for m in range(MEMBERS):
        low = ext[m, pl.ds(0, SLAB), pl.ds(0, LANES)]
        high = ext[m, pl.ds(0, SLAB), pl.ds(SEG - LANES, LANES)]
        edge = jnp.where(lane_tile < LANES // 2, low, high)
        mixed.append(edge)
        for n, at in enumerate((SLAB - 2, 0)):
            row_send[n, pl.ds(2 * m, 2), pl.ds(0, SEG)] = ext[m, pl.ds(at, 2), pl.ds(0, SEG)]
            row_send[n, pl.ds(2 * m, 2), pl.ds(SEG, LANES)] = edge[at : at + 2]
    columns = jnp.concatenate(mixed, axis=0).T
    col_send[0] = columns[LANES - 8 :]
    col_send[1] = columns[:8]


    finish = []

    def to_azi(n, src, dst, step):
        return pltpu.make_async_remote_copy(
            src_ref=src, dst_ref=dst, send_sem=send_sem.at[n], recv_sem=recv_sem.at[n],
            device_id={"rad": rad, "azi": lax.rem(azi + step, AZI)}, device_id_type=MESH,
        )

    def to_rad(n, src, dst, step):
        return pltpu.make_async_remote_copy(
            src_ref=src, dst_ref=dst, send_sem=send_sem.at[n], recv_sem=recv_sem.at[n],
            device_id={"rad": lax.rem(rad + step, RAD), "azi": azi}, device_id_type=MESH,
        )

    def every(count, make, begin=1, end=None):
        def one(step, carry):
            make(lax.rem(step + count // 2 - 2, count - 1) + 1).start()
            return carry

        lax.fori_loop(begin, end or count, one, 0)

    def rows(index, size=ROWS):
        return pl.ds(pl.multiple_of(index * size, 8), size)

    def wait_all(n, ref, sem):
        pltpu.make_async_copy(ref, ref, sem.at[n]).wait()

    def later(n, ref):
        finish.append(lambda: wait_all(n, ref, send_sem))

    def target(step):
        return lax.rem(azi + step, AZI)

    def ring(step):
        return lax.rem(rad + step, RAD)

    pl.semaphore_wait(barrier, AZI - 1 + RAD - 1 + 4)

    every(AZI, lambda s: to_azi(0, surf_out.at[:, target(s)], surf_in.at[:, azi], s))
    later(0, surf_in.at[:, pl.ds(1, AZI - 1)])
    for c in range(3):
        surf_in[c, azi] = surf_out[c, azi]

    def halo(n, src, dst, r_to, a_to):
        return pltpu.make_async_remote_copy(
            src_ref=src, dst_ref=dst, send_sem=halo_send.at[n], recv_sem=halo_recv.at[n],
            device_id={"rad": r_to, "azi": a_to}, device_id_type=MESH,
        )

    plain, corner = pl.ds(0, SEG), pl.ds(SEG, LANES)
    halos = [
        halo(0, row_send.at[0, :, plain], row_in.at[0], outer, azi),
        halo(1, row_send.at[1, :, plain], row_in.at[1], inner, azi),
        halo(2, col_send.at[0], col_in.at[pl.ds(LANES - 8, 8)], rad, right),
        halo(3, col_send.at[1], col_in.at[pl.ds(0, 8)], rad, left),
        halo(4, row_send.at[0, :, corner], tile_in.at[0], outer, right),
        halo(5, row_send.at[0, :, corner], tile_in.at[1], outer, left),
        halo(6, row_send.at[1, :, corner], tile_in.at[2], inner, right),
        halo(7, row_send.at[1, :, corner], tile_in.at[3], inner, left),
    ]
    for one in halos:
        one.start()
    finish += [one.wait_send for one in halos]
    for load in loads[3:6]:
        load.wait()
    wait_all(0, surf_in.at[:, pl.ds(1, AZI - 1)], recv_sem)
    sums = jnp.concatenate([surf_in[c].reshape(128, 128) for c in range(3)], axis=1)
    halves = dot(t_first[...], sums)
    joined = []
    for c in range(3):
        turn_cos, turn_sin = t_twiddle[:128], t_twiddle[128:]
        real, imag = halves[:128, 128 * c : 128 * (c + 1)], halves[128:, 128 * c : 128 * (c + 1)]
        joined.append(
            jnp.concatenate([real * turn_cos + imag * turn_sin, imag * turn_cos - real * turn_sin], axis=1)
        )
    modes = dot(jnp.concatenate(joined, axis=0), t_straight[...])
    own = iota((384, 256), 0) % 8 == iota((384, 256), 1) // 2 % 8
    pick = (iota((48, 384), 1) // 8 == iota((48, 384), 0)).astype(F32)
    modes = dot(pick, jnp.where(own, modes, 0.0))
    note = jnp.where(iota((1, LANES), 1) % 2 == 0, shift[azi].astype(F32), rest[azi])
    for h in range(2):
        for q in range(16):
            for c in range(3):
                spec_out[16 * h + q, c, :] = modes[16 * c + q, 128 * h : 128 * (h + 1)]
            spec_out[16 * h + q, 3, :] = note[0]
    every(AZI, lambda s: to_azi(2, spec_out.at[target(s)], spec_in.at[azi], s))
    later(2, spec_in.at[pl.ds(1, AZI - 1)])
    spec_in[azi] = spec_out[azi]

    for one in halos:
        one.wait_recv()

    sides = col_in[...].T
    lane_two = iota((2, LANES), 1)
    for m in range(MEMBERS):
        ext[m, pl.ds(0, SLAB), pl.ds(SEG, LANES)] = sides[SLAB * m : SLAB * (m + 1)]
    for m in range(MEMBERS):
        pair = pl.ds(2 * m, 2)
        for n, (at, edge_at, at_edge) in enumerate(
            ((EXT_R - 2, 0, rad == 0), (SLAB, SLAB - 1, rad == RAD - 1))
        ):
            edge = ext[m, pl.ds(edge_at, 1), :]
            far = jnp.where(lane_two < LANES // 2, tile_in[2 * n + 1, pair, :], tile_in[2 * n, pair, :])
            got = jnp.concatenate([row_in[n, pair, :], far], axis=1)
            ext[m, pl.ds(at, 2), :] = jnp.where(at_edge, jnp.broadcast_to(edge, (2, EXT_P)), got)

    coeffs = [wide(coef[n], EXT_P // LANES) for n in range(3)]
    for z in range(NZ):
        change, center = rates(lambda c, zz: ext[NZ * c + zz], z, EXT_R, coeffs)
        for c in range(3):
            sect[NZ * c + z] = center[c] + change[c]
    for m in range(MEMBERS):
        top = sect[m, pl.ds(0, 1), :]
        sect[m, pl.ds(EXT_R - 1, 1), :] = jnp.where(rad == 0, top, sect[m, pl.ds(EXT_R - 1, 1), :])
        low = sect[m, pl.ds(SLAB - 1, 1), :]
        sect[m, pl.ds(SLAB, 1), :] = jnp.where(rad == RAD - 1, low, sect[m, pl.ds(SLAB, 1), :])
    coeffs = [wide(coef[n, pl.ds(0, SLAB), :], EXT_P // LANES) for n in range(3)]
    weights = [weight[n] for n in range(4)]
    lower = {}
    for z in range(NZ):
        change, center = rates(lambda c, zz: sect[NZ * c + zz], z, SLAB, coeffs)
        for c in range(3):
            m = NZ * c + z
            hydro = 0.5 * ext[m, pl.ds(0, SLAB), :] + 0.5 * (center[c] + change[c])
            ahead = pltpu.roll(hydro, EXT_P - 1, 1)
            behind = pltpu.roll(hydro, 1, 1)
            behind_two = pltpu.roll(hydro, 2, 1)
            for quad in range(QUADS):
                lanes = slice(LANES * quad, LANES * (quad + 1))
                moved = (
                    weights[0] * ahead[:, lanes] + weights[1] * hydro[:, lanes]
                    + weights[2] * behind[:, lanes] + weights[3] * behind_two[:, lanes]
                )
                code = encode(moved)
                if z % 2 == 0:
                    lower[c, quad] = code & 0xFFFF
                    continue
                words = (code << 16) | lower[c, quad]
                for block in range(SLAB // 8):
                    at = 8 * ROWS * block + WORDS * quad + 2 * c + z // 2
                    move_out[pl.ds(at, 8, stride=ROWS), :] = words[8 * block : 8 * block + 8]

    def send_moves(begin, end):
        every(AZI, lambda s: to_azi(1, move_out.at[rows(target(s))], cycle_in.at[rows(azi)], s), begin, end)

    send_moves(1, FIRST_MOVES)
    cycle_in[rows(azi), :] = move_out[rows(azi), :]

    wait_all(2, spec_in.at[pl.ds(1, AZI - 1)], recv_sem)
    tile_lane = iota((AZI // 2, LANES), 1) // 16
    parts = [spec_in[pl.ds(16 * h, 16), c, :] for h in range(2) for c in range(4)]
    for n in range(RAD):
        packed = parts[0] if n == 0 else pltpu.roll(parts[0], LANES - 16 * n, 1)
        for at in range(1, 8):
            turn = 16 * (at - n) % LANES
            packed = jnp.where(tile_lane == at, pltpu.roll(parts[at], turn, 1) if turn else parts[at], packed)
        modes_out[n] = packed
    every(RAD, lambda s: to_rad(4, modes_out.at[ring(s)], modes_in.at[rad], s))
    later(4, modes_in.at[pl.ds(1, RAD - 1)])
    send_moves(FIRST_MOVES, AZI)
    later(1, cycle_in.at[pl.ds(0, ROWS * (AZI - 1))])
    modes_in[rad] = modes_out[rad]

    shape = (16, NR)
    mode = 256 * rad + 8 * azi + iota(shape, 0) // 2
    part = iota(shape, 0) % 2
    at_cycle = iota(shape, 1)
    theta = (2.0 * np.pi / NPHI) * mode.astype(F32)
    wave_cos, wave_sin = jnp.cos(theta), jnp.sin(theta)
    double_cos, double_sin = jnp.cos(2.0 * theta), jnp.sin(2.0 * theta)
    cycle_radius = 1.0 + 4.0 * (at_cycle.astype(F32) + 0.5) / NR
    cycle_steep = 1.0 / (cycle_radius * jnp.sqrt(cycle_radius))
    courant, coriolis, epicycle = 0.3 / cycle_radius, 0.2 * cycle_steep, 0.05 * cycle_steep
    drift = courant * wave_sin
    bend = 2.0 * wave_cos - 2.0

    def times_i(value):
        return jnp.where(part == 0, -pltpu.roll(value, 15, 0), pltpu.roll(value, 1, 0))

    def neighbours(value):
        behind = jnp.where(at_cycle == 0, value, pltpu.roll(value, 1, 1))
        ahead = jnp.where(at_cycle == NR - 1, value, pltpu.roll(value, NR - 1, 1))
        return 0.5 * (ahead - behind), (ahead + behind - 2.0 * value) + bend * value

    loads[6].wait()
    wait_all(4, modes_in.at[pl.ds(1, RAD - 1)], recv_sem)
    arrived = []
    for n in range(RAD):
        arrived += [modes_in[n], pltpu.roll(modes_in[n], LANES // 2, 1)]
    arrived = jnp.concatenate(arrived, axis=0).T
    rho, ur, up, extra = [arrived[16 * c : 16 * (c + 1)] for c in range(4)]
    cycle_turn = jnp.where(part == 0, extra, pltpu.roll(extra, 1, 0)).astype(jnp.int32)
    fraction = jnp.where(part == 0, pltpu.roll(extra, 15, 0), extra)
    phase = (2.0 * np.pi / NPHI) * ((mode * cycle_turn) & (NPHI - 1)).astype(F32)
    phase_cos, phase_sin = jnp.cos(phase), jnp.sin(phase)
    w_next, w_here, w_prev, w_prev_two = cubic_weights(fraction)
    mix_real = (w_next + w_prev) * wave_cos + w_here + w_prev_two * double_cos
    mix_imag = (w_next - w_prev) * wave_sin - w_prev_two * double_sin
    turn_real = mix_real * phase_cos + mix_imag * phase_sin
    turn_imag = mix_imag * phase_cos - mix_real * phase_sin
    rho_diff, rho_spread = neighbours(rho)
    ur_diff, ur_spread = neighbours(ur)
    rho_one = rho - (RADIAL_COURANT * ur_diff + drift * times_i(up)) + VISCOSITY * rho_spread
    ur_one = ur + coriolis * up - RADIAL_COURANT * rho_diff + VISCOSITY * ur_spread
    up_one = up - epicycle * ur - drift * times_i(rho) + VISCOSITY * neighbours(up)[1]
    change = VISCOSITY * neighbours(rho_one)[1] - (
        RADIAL_COURANT * neighbours(ur_one)[0] + drift * times_i(up_one)
    )
    surface = 0.5 * rho + 0.5 * (rho_one + change)
    spectrum = (turn_real * surface + turn_imag * times_i(surface)).astype(jnp.bfloat16)

    mode_potential = jnp.zeros(shape, F32)
    for k in range(8):
        product = lax.dot_general(
            spectrum, kern[k], (((1,), (1,)), ((), ())), preferred_element_type=F32
        )
        mode_potential = jnp.where(iota(shape, 0) // 2 == k, product, mode_potential)
    for h in range(2):
        pot_out[h] = mode_potential[:, LANES * h : LANES * (h + 1)]
    every(RAD, lambda s: to_rad(5, pot_out.at[ring(s) // 4], pot_in.at[rad], s))
    later(5, pot_in.at[pl.ds(1, RAD - 1)])
    pot_in[rad] = pot_out[rad // 4]
    wait_all(1, cycle_in.at[pl.ds(0, ROWS * (AZI - 1))], recv_sem)
    cycle_in[pl.ds(ROWS * AZI, ROWS), :] = cycle_in[pl.ds(0, ROWS), :]
    my_shift = shift[azi]
    turn_rows, turn_lanes = my_shift // LANES, my_shift % LANES
    lane = iota((ROWS, LANES), 1)

    def rotated(segment):
        start = lax.rem(QUADS * segment + LANES - 1 - turn_rows + LANES, LANES) * WORDS
        here = cycle_in[pl.ds(start + WORDS, ROWS), :]
        before = cycle_in[pl.ds(start, ROWS), :]
        return pltpu.roll(jnp.where(lane < LANES - turn_lanes, here, before), turn_lanes, 1)

    def rotate_and_send(step, carry):
        step = lax.rem(step + AZI // 2 - 2, AZI - 1) + 1
        segment = target(step)
        cycle_out[rows(segment), :] = rotated(segment)
        to_azi(3, cycle_out.at[rows(segment)], move_in.at[rows(azi)], step).start()
        return carry

    lax.fori_loop(1, AZI, rotate_and_send, 0)
    later(3, move_in.at[pl.ds(0, ROWS * (AZI - 1))])
    move_in[rows(azi), :] = rotated(azi)

    wait_all(5, pot_in.at[pl.ds(1, RAD - 1)], recv_sem)
    lines[...] = pot_in[...].reshape(LANES, LANES).T
    gathered = lines[rows(lax.rem(rad, 4), SLAB), :]
    for n in range(SLAB):
        back_out[n, 0, :] = gathered[n]
    every(AZI, lambda s: to_azi(6, back_out.at[target(s)], back_in.at[azi], s))
    later(6, back_in.at[pl.ds(1, AZI - 1)])
    back_in[azi] = back_out[azi]
    wait_all(3, move_in.at[pl.ds(0, ROWS * (AZI - 1))], recv_sem)
    for c, out in enumerate((density_out, radial_out, azimuthal_out)):
        for pair in range(NZ // 2):
            for quad in range(QUADS):
                for block in range(SLAB // 8):
                    at = 8 * ROWS * block + WORDS * quad + 2 * c + pair
                    words = move_in[pl.ds(at, 8, stride=ROWS), :]
                    place = pl.ds(8 * block, 8), pl.ds(LANES * quad, LANES)
                    out[2 * pair, *place] = decode((words << 16) >> 16)
                    out[2 * pair + 1, *place] = decode(words >> 16)

    for load in loads[7:9]:
        load.wait()
    wait_all(6, back_in.at[pl.ds(1, AZI - 1)], recv_sem)
    values = back_in[:, 0, :]
    values = jnp.concatenate([values[:16], values[16:]], axis=1)
    spread = (iota((128, 16), 0) // 8 == iota((128, 16), 1)).astype(F32)
    zero_mode = (iota((128, 256), 0) == 0) & (iota((128, 256), 1) < 2)
    own = iota((128, 256), 0) % 8 == iota((128, 256), 1) // 2 % 8
    values = jnp.where(own, dot(spread, values) * jnp.where(zero_mode, 1.0 / NPHI, 2.0 / NPHI), 0.0)
    pieces = dot(values, t_back[...])
    real, imag = pieces[:, :128], pieces[:, 128:]
    turn_cos, turn_sin = t_twiddle[:128], t_twiddle[128:]
    joined = jnp.concatenate([real * turn_cos - imag * turn_sin, real * turn_sin + imag * turn_cos], axis=0)
    potential[...] = dot(t_last[...], joined)


    for wait in finish:
        wait()


def unload(*refs):
    pairs, sems = zip(refs[:4], refs[4:8]), refs[8]
    copies = [pltpu.make_async_copy(src, dst, sems.at[n]) for n, (src, dst) in enumerate(pairs)]
    for copy in copies:
        copy.start()
    for copy in copies:
        copy.wait()


def step(density, radial_velocity, azimuthal_velocity, cycle_shift, remainder, kernel):
    whole = pl.BlockSpec(memory_space=pltpu.VMEM)
    away = pl.BlockSpec(memory_space=pltpu.HBM)
    shapes = [jax.ShapeDtypeStruct((NZ, SLAB, SEG), F32)] * 3 + [jax.ShapeDtypeStruct((128, 128), F32)]
    moves = pltpu.VMEM((ROWS * AZI, LANES), jnp.int32)
    single = pltpu.VMEM((AZI, 1, LANES), F32)
    results = pl.pallas_call(
        body,
        name="disc_step",
        out_shape=shapes,
        in_specs=[away] * 11,
        out_specs=[whole] * 4,
        scratch_shapes=[
            pltpu.VMEM((MEMBERS, EXT_R, EXT_P), F32),
            pltpu.VMEM((MEMBERS, EXT_R, EXT_P), F32),
            pltpu.VMEM((3, EXT_R, LANES), F32),
            pltpu.VMEM((4, SLAB, LANES), F32),
            pltpu.VMEM((2, 2 * MEMBERS, EXT_P), F32),
            pltpu.VMEM((2, 2 * MEMBERS, SEG), F32),
            pltpu.VMEM((4, 2 * MEMBERS, LANES), F32),
            pltpu.VMEM((2, 8, MEMBERS * SLAB), F32),
            pltpu.VMEM((LANES, MEMBERS * SLAB), F32),
            moves,
            pltpu.VMEM((ROWS * (AZI + 1), LANES), jnp.int32),
            moves,
            moves,
            pltpu.VMEM((3, AZI, QUADS, LANES), F32),
            pltpu.VMEM((3, AZI, QUADS, LANES), F32),
            pltpu.VMEM((AZI, 4, LANES), F32),
            pltpu.VMEM((AZI, 4, LANES), F32),
            pltpu.VMEM((RAD, AZI // 2, LANES), F32),
            pltpu.VMEM((RAD, AZI // 2, LANES), F32),
            pltpu.VMEM((2, 16, LANES), F32),
            pltpu.VMEM((RAD, 16, LANES), F32),
            pltpu.VMEM((LANES, LANES), F32),
            single,
            single,
            pltpu.VMEM((8, NR, NR), jnp.bfloat16),
            pltpu.VMEM((256, 128), F32),
            pltpu.VMEM((128, 256), F32),
            pltpu.VMEM((256, 128), F32),
            pltpu.VMEM((256, 256), F32),
            pltpu.VMEM((256, 256), F32),
            pltpu.SMEM((SLAB,), jnp.int32),
            pltpu.SMEM((SLAB,), F32),
            pltpu.SemaphoreType.DMA((11,)),
            pltpu.SemaphoreType.DMA((8,)),
            pltpu.SemaphoreType.DMA((8,)),
            pltpu.SemaphoreType.DMA((7,)),
            pltpu.SemaphoreType.DMA((7,)),
        ],
        compiler_params=pltpu.CompilerParams(
            collective_id=0, has_side_effects=True, vmem_limit_bytes=40 * 1024 * 1024
        ),
    )(
        *[
            pltpu.with_memory_space_constraint(value, pltpu.HBM)
            for value in (
                density, radial_velocity, azimuthal_velocity, cycle_shift, remainder, kernel,
                *[jnp.asarray(table) for table in tables()],
            )
        ]
    )
    *fields, potential = pl.pallas_call(
        unload,
        name="unload",
        out_shape=shapes,
        in_specs=[whole] * 4,
        out_specs=[pl.BlockSpec(memory_space=pl.ANY)] * 4,
        scratch_shapes=[pltpu.SemaphoreType.DMA((4,))],
        compiler_params=pltpu.CompilerParams(vmem_limit_bytes=8 * 1024 * 1024),
    )(*results)
    return *fields, potential.reshape(1, NPHI)


def solution(mesh):
    field = P(None, "rad", "azi")
    both = P(("rad", "azi"), None)
    return jax.shard_map(
        step,
        mesh=mesh,
        in_specs=(field, field, field, P("rad"), P("rad"), P(("rad", "azi"), None, None)),
        out_specs=(field, field, field, both),
        check_vma=False,
    )
```

```python
import numpy as np

import jax
import jax.numpy as jnp
from jax import lax
from jax.experimental import pallas as pl
from jax.experimental.pallas import tpu as pltpu
from jax.sharding import PartitionSpec as P

NZ = 4
NPHI = 16384
MODES = 2048
NR = 256
RAD = 8
AZI = 32
SLAB = NR // RAD
SEG = NPHI // AZI
LANES = 128
QUADS = SEG // LANES
MEMBERS = 3 * NZ
WORDS = MEMBERS // 2
ROWS = WORDS * QUADS
FIRST_MOVES = 9
CODES = 32767
OCTAVES = 28.0
TOP = 4.0
EXT_R = SLAB + 8
EXT_P = SEG + LANES
RADIAL_COURANT = 0.3
VISCOSITY = 0.08
HIGHEST = lax.Precision.HIGHEST
F32 = jnp.float32
MESH = pl.DeviceIdType.MESH


def tables():
    n = np.arange(128)
    turn = 2.0 * np.pi / 128 * (np.outer(n, n) % 128)
    first = np.concatenate([np.cos(turn), -np.sin(turn)], axis=0)
    last = np.concatenate([np.cos(turn), -np.sin(turn)], axis=1)
    small = 2.0 * np.pi / NPHI * np.outer(n, n)
    twiddle = np.concatenate([np.cos(small), np.sin(small)], axis=0)
    col = np.arange(256)
    half, ring, part = col // 128, col % 128 // 16, col % 2
    phi = 2.0 * np.pi / 128 * (np.outer(n, 2 * ring + half) % 128)
    cos, sin = np.cos(phi), np.sin(phi)
    real = part == 0
    straight = np.concatenate([np.where(real, cos, -sin), np.where(real, sin, cos)], axis=0)
    real = real[:, None]
    back = np.concatenate(
        [np.where(real, cos.T, -sin.T), np.where(real, sin.T, cos.T)], axis=1
    )
    pairs = []
    for table in (last, back):
        high = table.astype(jnp.bfloat16)
        pairs.append(np.stack([high, (table - high.astype(np.float64)).astype(jnp.bfloat16)]))
    return [t.astype(np.float32) for t in (first, twiddle, straight)] + pairs


def dot(left, right):
    return jnp.dot(left, right, precision=HIGHEST, preferred_element_type=F32)


def halves_of(value):
    high = value.astype(jnp.bfloat16)
    return high, (value - high.astype(F32)).astype(jnp.bfloat16)


def dot_split(left, right):
    def part(a, b):
        return jnp.dot(a, b, preferred_element_type=F32)

    return part(left[0], right[0]) + (part(left[0], right[1]) + part(left[1], right[0]))


def iota(shape, axis):
    return lax.broadcasted_iota(jnp.int32, shape, axis)


def wide(value, count):
    return jnp.concatenate([value] * count, axis=1)


def cubic_weights(remainder):
    moved = -remainder
    w_next = moved * (moved + 1.0) * (moved + 2.0) / 6.0
    w_here = -(moved - 1.0) * (moved + 1.0) * (moved + 2.0) / 2.0
    w_prev = (moved - 1.0) * moved * (moved + 2.0) / 2.0
    w_prev_two = -(moved - 1.0) * moved * (moved + 1.0) / 6.0
    return w_next, w_here, w_prev, w_prev_two


def encode(value):
    level = (jnp.log(jnp.abs(value)) * (1.0 / np.log(2.0)) - TOP) * (CODES / OCTAVES) + (CODES + 0.5)
    code = jnp.clip(level, 0.0, CODES + 0.5).astype(jnp.int32)
    return jnp.where(value < 0, -code, code)


def decode(code):
    level = (jnp.abs(code) - CODES).astype(F32) * (OCTAVES / CODES) + TOP
    size = jnp.where(code == 0, 0.0, jnp.exp(level * np.log(2.0)))
    return jnp.where(code < 0, -size, size)


def rates(get, z, rows, coeffs):
    courant, coriolis, epicycle = coeffs
    below, above = max(z - 1, 0), min(z + 1, NZ - 1)
    center, ahead, rad_diff, azi_diff, spread = [], [], [], [], []
    for c in range(3):
        whole = get(c, z)
        inner = pltpu.roll(whole, 1, 0)[:rows]
        outer = pltpu.roll(whole, EXT_R - 1, 0)[:rows]
        mid = whole[:rows]
        prev = pltpu.roll(mid, 1, 1)
        following = pltpu.roll(mid, EXT_P - 1, 1)
        center.append(mid)
        rad_diff.append(outer - inner if c < 2 else None)
        azi_diff.append(following - prev if c != 1 else None)
        total = (get(c, below)[:rows] + get(c, above)[:rows]) + (inner + outer) + (prev + following)
        spread.append(VISCOSITY * (total - 6.0 * mid))
    half = 0.5 * RADIAL_COURANT
    change = (
        spread[0] - (half * rad_diff[1] + courant * azi_diff[2]),
        spread[1] + coriolis * center[2] - half * rad_diff[0],
        spread[2] - epicycle * center[1] - courant * azi_diff[0],
    )
    return change, center


def body(
    density, radial_velocity, azimuthal_velocity, shift_far, rest_far, kernel, first, twiddle, straight, last,
    back, density_out, radial_out, azimuthal_out, potential,
    ext, sect, coef, weight, row_send, row_in, tile_in, col_send, col_in, move_out, cycle_in, cycle_out,
    move_in, surf_out, surf_in, spec_out, spec_in, modes_out, modes_in, pot_out, pot_in, lines, back_out,
    back_in, kern, t_first, t_last, t_twiddle, t_straight, t_back,
    shift, rest, local_sem, halo_send, halo_recv, send_sem, recv_sem,
):
    rad, azi = lax.axis_index("rad"), lax.axis_index("azi")
    outer, inner = lax.rem(rad + 1, RAD), lax.rem(rad + RAD - 1, RAD)
    right, left = lax.rem(azi + 1, AZI), lax.rem(azi + AZI - 1, AZI)

    loads = [
        pltpu.make_async_copy(src, ext.at[pl.ds(NZ * c, NZ), pl.ds(0, SLAB), pl.ds(0, SEG)], local_sem.at[c])
        for c, src in enumerate((density, radial_velocity, azimuthal_velocity))
    ]
    for n, (src, dst) in enumerate(
        (
            (first, t_first), (twiddle, t_twiddle), (straight, t_straight),
            (kernel, kern), (back, t_back), (last, t_last), (shift_far, shift), (rest_far, rest),
        )
    ):
        loads.append(pltpu.make_async_copy(src, dst, local_sem.at[3 + n]))
    for load in loads:
        load.start()

    col_in[...] = jnp.zeros(col_in.shape, F32)
    barrier = pltpu.get_barrier_semaphore()

    def greet_azi(step, carry):
        pl.semaphore_signal(
            barrier, inc=1, device_id={"rad": rad, "azi": lax.rem(azi + step, AZI)}, device_id_type=MESH
        )
        return carry

    def greet_rad(step, carry):
        pl.semaphore_signal(
            barrier, inc=1, device_id={"rad": lax.rem(rad + step, RAD), "azi": azi}, device_id_type=MESH
        )
        return carry

    for r_to in (outer, inner):
        for a_to in (right, left):
            pl.semaphore_signal(barrier, inc=1, device_id={"rad": r_to, "azi": a_to}, device_id_type=MESH)
    lax.fori_loop(1, AZI, greet_azi, 0)
    lax.fori_loop(1, RAD, greet_rad, 0)

    row = iota((EXT_R, LANES), 0)
    cycle = SLAB * rad + jnp.where(row < SLAB + 4, row, row - EXT_R)
    radius = 1.0 + 4.0 * (cycle.astype(F32) + 0.5) / NR
    steep = 1.0 / (radius * jnp.sqrt(radius))
    coef[0] = 0.15 / radius
    coef[1] = 0.2 * steep
    coef[2] = 0.05 * steep
    for load in loads[9:]:
        load.wait()
    block_row = iota((8, LANES), 0)
    for block in range(SLAB // 8):
        fraction = jnp.zeros((8, LANES), F32)
        for n in range(8):
            fraction = jnp.where(block_row == n, rest[8 * block + n], fraction)
        for n, value in enumerate(cubic_weights(fraction)):
            weight[n, pl.ds(8 * block, 8), :] = value
    ext[:, pl.ds(SLAB, 8), :] = jnp.zeros((MEMBERS, 8, EXT_P), F32)

    for load in loads[:3]:
        load.wait()
    for c in range(3):
        heights = [ext[NZ * c + z, pl.ds(0, SLAB), pl.ds(0, SEG)] for z in range(NZ)]
        total = (heights[0] + heights[1]) + (heights[2] + heights[3])
        for n in range(SLAB):
            for quad in range(QUADS):
                surf_out[c, n, quad, :] = total[n, LANES * quad : LANES * (quad + 1)]

    lane_tile = iota((SLAB, LANES), 1)
    mixed = []
    for m in range(MEMBERS):
        low = ext[m, pl.ds(0, SLAB), pl.ds(0, LANES)]
        high = ext[m, pl.ds(0, SLAB), pl.ds(SEG - LANES, LANES)]
        edge = jnp.where(lane_tile < LANES // 2, low, high)
        mixed.append(edge)
        for n, at in enumerate((SLAB - 2, 0)):
            row_send[n, pl.ds(2 * m, 2), pl.ds(0, SEG)] = ext[m, pl.ds(at, 2), pl.ds(0, SEG)]
            row_send[n, pl.ds(2 * m, 2), pl.ds(SEG, LANES)] = edge[at : at + 2]
    columns = jnp.concatenate(mixed, axis=0).T
    col_send[0] = columns[LANES - 8 :]
    col_send[1] = columns[:8]


    finish = []

    def to_azi(n, src, dst, step):
        return pltpu.make_async_remote_copy(
            src_ref=src, dst_ref=dst, send_sem=send_sem.at[n], recv_sem=recv_sem.at[n],
            device_id={"rad": rad, "azi": lax.rem(azi + step, AZI)}, device_id_type=MESH,
        )

    def to_rad(n, src, dst, step):
        return pltpu.make_async_remote_copy(
            src_ref=src, dst_ref=dst, send_sem=send_sem.at[n], recv_sem=recv_sem.at[n],
            device_id={"rad": lax.rem(rad + step, RAD), "azi": azi}, device_id_type=MESH,
        )

    def every(count, make, begin=1, end=None):
        def one(step, carry):
            make(lax.rem(step + count // 2 - 2, count - 1) + 1).start()
            return carry

        lax.fori_loop(begin, end or count, one, 0)

    def rows(index, size=ROWS):
        return pl.ds(pl.multiple_of(index * size, 8), size)

    def wait_all(n, ref, sem):
        pltpu.make_async_copy(ref, ref, sem.at[n]).wait()

    def later(n, ref):
        finish.append(lambda: wait_all(n, ref, send_sem))

    def target(step):
        return lax.rem(azi + step, AZI)

    def ring(step):
        return lax.rem(rad + step, RAD)

    pl.semaphore_wait(barrier, AZI - 1 + RAD - 1 + 4)

    every(AZI, lambda s: to_azi(0, surf_out.at[:, target(s)], surf_in.at[:, azi], s))
    later(0, surf_in.at[:, pl.ds(1, AZI - 1)])
    for c in range(3):
        surf_in[c, azi] = surf_out[c, azi]

    def halo(n, src, dst, r_to, a_to):
        return pltpu.make_async_remote_copy(
            src_ref=src, dst_ref=dst, send_sem=halo_send.at[n], recv_sem=halo_recv.at[n],
            device_id={"rad": r_to, "azi": a_to}, device_id_type=MESH,
        )

    plain, corner = pl.ds(0, SEG), pl.ds(SEG, LANES)
    halos = [
        halo(0, row_send.at[0, :, plain], row_in.at[0], outer, azi),
        halo(1, row_send.at[1, :, plain], row_in.at[1], inner, azi),
        halo(2, col_send.at[0], col_in.at[pl.ds(LANES - 8, 8)], rad, right),
        halo(3, col_send.at[1], col_in.at[pl.ds(0, 8)], rad, left),
        halo(4, row_send.at[0, :, corner], tile_in.at[0], outer, right),
        halo(5, row_send.at[0, :, corner], tile_in.at[1], outer, left),
        halo(6, row_send.at[1, :, corner], tile_in.at[2], inner, right),
        halo(7, row_send.at[1, :, corner], tile_in.at[3], inner, left),
    ]
    for one in halos:
        one.start()
    finish += [one.wait_send for one in halos]
    for load in loads[3:6]:
        load.wait()
    wait_all(0, surf_in.at[:, pl.ds(1, AZI - 1)], recv_sem)
    sums = jnp.concatenate([surf_in[c].reshape(128, 128) for c in range(3)], axis=1)
    halves = dot(t_first[...], sums)
    joined = []
    for c in range(3):
        turn_cos, turn_sin = t_twiddle[:128], t_twiddle[128:]
        real, imag = halves[:128, 128 * c : 128 * (c + 1)], halves[128:, 128 * c : 128 * (c + 1)]
        joined.append(
            jnp.concatenate([real * turn_cos + imag * turn_sin, imag * turn_cos - real * turn_sin], axis=1)
        )
    modes = dot(jnp.concatenate(joined, axis=0), t_straight[...])
    own = iota((384, 256), 0) % 8 == iota((384, 256), 1) // 2 % 8
    pick = (iota((48, 384), 1) // 8 == iota((48, 384), 0)).astype(F32)
    modes = dot(pick, jnp.where(own, modes, 0.0))
    note = jnp.where(iota((1, LANES), 1) % 2 == 0, shift[azi].astype(F32), rest[azi])
    for h in range(2):
        for q in range(16):
            for c in range(3):
                spec_out[16 * h + q, c, :] = modes[16 * c + q, 128 * h : 128 * (h + 1)]
            spec_out[16 * h + q, 3, :] = note[0]
    every(AZI, lambda s: to_azi(2, spec_out.at[target(s)], spec_in.at[azi], s))
    later(2, spec_in.at[pl.ds(1, AZI - 1)])
    spec_in[azi] = spec_out[azi]

    for one in halos:
        one.wait_recv()

    sides = col_in[...].T
    lane_two = iota((2, LANES), 1)
    for m in range(MEMBERS):
        ext[m, pl.ds(0, SLAB), pl.ds(SEG, LANES)] = sides[SLAB * m : SLAB * (m + 1)]
    for m in range(MEMBERS):
        pair = pl.ds(2 * m, 2)
        for n, (at, edge_at, at_edge) in enumerate(
            ((EXT_R - 2, 0, rad == 0), (SLAB, SLAB - 1, rad == RAD - 1))
        ):
            edge = ext[m, pl.ds(edge_at, 1), :]
            far = jnp.where(lane_two < LANES // 2, tile_in[2 * n + 1, pair, :], tile_in[2 * n, pair, :])
            got = jnp.concatenate([row_in[n, pair, :], far], axis=1)
            ext[m, pl.ds(at, 2), :] = jnp.where(at_edge, jnp.broadcast_to(edge, (2, EXT_P)), got)

    coeffs = [wide(coef[n], EXT_P // LANES) for n in range(3)]
    for z in range(NZ):
        change, center = rates(lambda c, zz: ext[NZ * c + zz], z, EXT_R, coeffs)
        for c in range(3):
            sect[NZ * c + z] = center[c] + change[c]
    for m in range(MEMBERS):
        top = sect[m, pl.ds(0, 1), :]
        sect[m, pl.ds(EXT_R - 1, 1), :] = jnp.where(rad == 0, top, sect[m, pl.ds(EXT_R - 1, 1), :])
        low = sect[m, pl.ds(SLAB - 1, 1), :]
        sect[m, pl.ds(SLAB, 1), :] = jnp.where(rad == RAD - 1, low, sect[m, pl.ds(SLAB, 1), :])
    coeffs = [wide(coef[n, pl.ds(0, SLAB), :], EXT_P // LANES) for n in range(3)]
    weights = [weight[n] for n in range(4)]
    lower = {}
    for z in range(NZ):
        change, center = rates(lambda c, zz: sect[NZ * c + zz], z, SLAB, coeffs)
        for c in range(3):
            m = NZ * c + z
            hydro = 0.5 * ext[m, pl.ds(0, SLAB), :] + 0.5 * (center[c] + change[c])
            ahead = pltpu.roll(hydro, EXT_P - 1, 1)
            behind = pltpu.roll(hydro, 1, 1)
            behind_two = pltpu.roll(hydro, 2, 1)
            for quad in range(QUADS):
                lanes = slice(LANES * quad, LANES * (quad + 1))
                moved = (
                    weights[0] * ahead[:, lanes] + weights[1] * hydro[:, lanes]
                    + weights[2] * behind[:, lanes] + weights[3] * behind_two[:, lanes]
                )
                code = encode(moved)
                if z % 2 == 0:
                    lower[c, quad] = code & 0xFFFF
                    continue
                words = (code << 16) | lower[c, quad]
                for block in range(SLAB // 8):
                    at = 8 * ROWS * block + WORDS * quad + 2 * c + z // 2
                    move_out[pl.ds(at, 8, stride=ROWS), :] = words[8 * block : 8 * block + 8]

    def send_moves(begin, end):
        every(AZI, lambda s: to_azi(1, move_out.at[rows(target(s))], cycle_in.at[rows(azi)], s), begin, end)

    send_moves(1, FIRST_MOVES)
    cycle_in[rows(azi), :] = move_out[rows(azi), :]

    wait_all(2, spec_in.at[pl.ds(1, AZI - 1)], recv_sem)
    tile_lane = iota((AZI // 2, LANES), 1) // 16
    parts = [spec_in[pl.ds(16 * h, 16), c, :] for h in range(2) for c in range(4)]
    for n in range(RAD):
        packed = parts[0] if n == 0 else pltpu.roll(parts[0], LANES - 16 * n, 1)
        for at in range(1, 8):
            turn = 16 * (at - n) % LANES
            packed = jnp.where(tile_lane == at, pltpu.roll(parts[at], turn, 1) if turn else parts[at], packed)
        modes_out[n] = packed
    every(RAD, lambda s: to_rad(4, modes_out.at[ring(s)], modes_in.at[rad], s))
    later(4, modes_in.at[pl.ds(1, RAD - 1)])
    send_moves(FIRST_MOVES, AZI)
    later(1, cycle_in.at[pl.ds(0, ROWS * (AZI - 1))])
    modes_in[rad] = modes_out[rad]

    shape = (16, NR)
    mode = 256 * rad + 8 * azi + iota(shape, 0) // 2
    part = iota(shape, 0) % 2
    at_cycle = iota(shape, 1)
    theta = (2.0 * np.pi / NPHI) * mode.astype(F32)
    wave_cos, wave_sin = jnp.cos(theta), jnp.sin(theta)
    double_cos, double_sin = jnp.cos(2.0 * theta), jnp.sin(2.0 * theta)
    cycle_radius = 1.0 + 4.0 * (at_cycle.astype(F32) + 0.5) / NR
    cycle_steep = 1.0 / (cycle_radius * jnp.sqrt(cycle_radius))
    courant, coriolis, epicycle = 0.3 / cycle_radius, 0.2 * cycle_steep, 0.05 * cycle_steep
    drift = courant * wave_sin
    bend = 2.0 * wave_cos - 2.0

    def times_i(value):
        return jnp.where(part == 0, -pltpu.roll(value, 15, 0), pltpu.roll(value, 1, 0))

    def neighbours(value):
        behind = jnp.where(at_cycle == 0, value, pltpu.roll(value, 1, 1))
        ahead = jnp.where(at_cycle == NR - 1, value, pltpu.roll(value, NR - 1, 1))
        return 0.5 * (ahead - behind), (ahead + behind - 2.0 * value) + bend * value

    loads[6].wait()
    wait_all(4, modes_in.at[pl.ds(1, RAD - 1)], recv_sem)
    arrived = []
    for n in range(RAD):
        arrived += [modes_in[n], pltpu.roll(modes_in[n], LANES // 2, 1)]
    arrived = jnp.concatenate(arrived, axis=0).T
    rho, ur, up, extra = [arrived[16 * c : 16 * (c + 1)] for c in range(4)]
    cycle_turn = jnp.where(part == 0, extra, pltpu.roll(extra, 1, 0)).astype(jnp.int32)
    fraction = jnp.where(part == 0, pltpu.roll(extra, 15, 0), extra)
    phase = (2.0 * np.pi / NPHI) * ((mode * cycle_turn) & (NPHI - 1)).astype(F32)
    phase_cos, phase_sin = jnp.cos(phase), jnp.sin(phase)
    w_next, w_here, w_prev, w_prev_two = cubic_weights(fraction)
    mix_real = (w_next + w_prev) * wave_cos + w_here + w_prev_two * double_cos
    mix_imag = (w_next - w_prev) * wave_sin - w_prev_two * double_sin
    turn_real = mix_real * phase_cos + mix_imag * phase_sin
    turn_imag = mix_imag * phase_cos - mix_real * phase_sin
    rho_diff, rho_spread = neighbours(rho)
    ur_diff, ur_spread = neighbours(ur)
    rho_one = rho - (RADIAL_COURANT * ur_diff + drift * times_i(up)) + VISCOSITY * rho_spread
    ur_one = ur + coriolis * up - RADIAL_COURANT * rho_diff + VISCOSITY * ur_spread
    up_one = up - epicycle * ur - drift * times_i(rho) + VISCOSITY * neighbours(up)[1]
    change = VISCOSITY * neighbours(rho_one)[1] - (
        RADIAL_COURANT * neighbours(ur_one)[0] + drift * times_i(up_one)
    )
    surface = 0.5 * rho + 0.5 * (rho_one + change)
    spectrum = (turn_real * surface + turn_imag * times_i(surface)).astype(jnp.bfloat16)

    mode_potential = jnp.zeros(shape, F32)
    for k in range(8):
        product = lax.dot_general(
            spectrum, kern[k], (((1,), (1,)), ((), ())), preferred_element_type=F32
        )
        mode_potential = jnp.where(iota(shape, 0) // 2 == k, product, mode_potential)
    for h in range(2):
        pot_out[h] = mode_potential[:, LANES * h : LANES * (h + 1)]
    every(RAD, lambda s: to_rad(5, pot_out.at[ring(s) // 4], pot_in.at[rad], s))
    later(5, pot_in.at[pl.ds(1, RAD - 1)])
    pot_in[rad] = pot_out[rad // 4]
    wait_all(1, cycle_in.at[pl.ds(0, ROWS * (AZI - 1))], recv_sem)
    cycle_in[pl.ds(ROWS * AZI, ROWS), :] = cycle_in[pl.ds(0, ROWS), :]
    my_shift = shift[azi]
    turn_rows, turn_lanes = my_shift // LANES, my_shift % LANES
    lane = iota((ROWS, LANES), 1)

    def rotated(segment):
        start = lax.rem(QUADS * segment + LANES - 1 - turn_rows + LANES, LANES) * WORDS
        here = cycle_in[pl.ds(start + WORDS, ROWS), :]
        before = cycle_in[pl.ds(start, ROWS), :]
        return pltpu.roll(jnp.where(lane < LANES - turn_lanes, here, before), turn_lanes, 1)

    def rotate_and_send(step, carry):
        step = lax.rem(step + AZI // 2 - 2, AZI - 1) + 1
        segment = target(step)
        cycle_out[rows(segment), :] = rotated(segment)
        to_azi(3, cycle_out.at[rows(segment)], move_in.at[rows(azi)], step).start()
        return carry

    lax.fori_loop(1, AZI, rotate_and_send, 0)
    later(3, move_in.at[pl.ds(0, ROWS * (AZI - 1))])
    move_in[rows(azi), :] = rotated(azi)

    wait_all(5, pot_in.at[pl.ds(1, RAD - 1)], recv_sem)
    lines[...] = pot_in[...].reshape(LANES, LANES).T
    gathered = lines[rows(lax.rem(rad, 4), SLAB), :]
    for n in range(SLAB):
        back_out[n, 0, :] = gathered[n]
    every(AZI, lambda s: to_azi(6, back_out.at[target(s)], back_in.at[azi], s))
    later(6, back_in.at[pl.ds(1, AZI - 1)])
    back_in[azi] = back_out[azi]
    wait_all(3, move_in.at[pl.ds(0, ROWS * (AZI - 1))], recv_sem)
    for c, out in enumerate((density_out, radial_out, azimuthal_out)):
        for pair in range(NZ // 2):
            for quad in range(QUADS):
                for block in range(SLAB // 8):
                    at = 8 * ROWS * block + WORDS * quad + 2 * c + pair
                    words = move_in[pl.ds(at, 8, stride=ROWS), :]
                    place = pl.ds(8 * block, 8), pl.ds(LANES * quad, LANES)
                    out[2 * pair, *place] = decode((words << 16) >> 16)
                    out[2 * pair + 1, *place] = decode(words >> 16)

    for load in loads[7:9]:
        load.wait()
    wait_all(6, back_in.at[pl.ds(1, AZI - 1)], recv_sem)
    values = back_in[:, 0, :]
    values = jnp.concatenate([values[:16], values[16:]], axis=1)
    spread = (iota((128, 16), 0) // 8 == iota((128, 16), 1)).astype(F32).astype(jnp.bfloat16)
    high, low = [jnp.dot(spread, piece, preferred_element_type=F32) for piece in halves_of(values)]
    zero_mode = (iota((128, 256), 0) == 0) & (iota((128, 256), 1) < 2)
    own = iota((128, 256), 0) % 8 == iota((128, 256), 1) // 2 % 8
    values = jnp.where(own, (high + low) * jnp.where(zero_mode, 1.0 / NPHI, 2.0 / NPHI), 0.0)
    pieces = dot_split(halves_of(values), (t_back[0], t_back[1]))
    real, imag = pieces[:, :128], pieces[:, 128:]
    turn_cos, turn_sin = t_twiddle[:128], t_twiddle[128:]
    joined = jnp.concatenate([real * turn_cos - imag * turn_sin, real * turn_sin + imag * turn_cos], axis=0)
    potential[...] = dot_split((t_last[0], t_last[1]), halves_of(joined))


    for wait in finish:
        wait()


def unload(*refs):
    pairs, sems = zip(refs[:4], refs[4:8]), refs[8]
    copies = [pltpu.make_async_copy(src, dst, sems.at[n]) for n, (src, dst) in enumerate(pairs)]
    for copy in copies:
        copy.start()
    for copy in copies:
        copy.wait()


def step(density, radial_velocity, azimuthal_velocity, cycle_shift, remainder, kernel):
    whole = pl.BlockSpec(memory_space=pltpu.VMEM)
    away = pl.BlockSpec(memory_space=pltpu.HBM)
    shapes = [jax.ShapeDtypeStruct((NZ, SLAB, SEG), F32)] * 3 + [jax.ShapeDtypeStruct((128, 128), F32)]
    moves = pltpu.VMEM((ROWS * AZI, LANES), jnp.int32)
    single = pltpu.VMEM((AZI, 1, LANES), F32)
    results = pl.pallas_call(
        body,
        name="disc_step",
        out_shape=shapes,
        in_specs=[away] * 11,
        out_specs=[whole] * 4,
        scratch_shapes=[
            pltpu.VMEM((MEMBERS, EXT_R, EXT_P), F32),
            pltpu.VMEM((MEMBERS, EXT_R, EXT_P), F32),
            pltpu.VMEM((3, EXT_R, LANES), F32),
            pltpu.VMEM((4, SLAB, LANES), F32),
            pltpu.VMEM((2, 2 * MEMBERS, EXT_P), F32),
            pltpu.VMEM((2, 2 * MEMBERS, SEG), F32),
            pltpu.VMEM((4, 2 * MEMBERS, LANES), F32),
            pltpu.VMEM((2, 8, MEMBERS * SLAB), F32),
            pltpu.VMEM((LANES, MEMBERS * SLAB), F32),
            moves,
            pltpu.VMEM((ROWS * (AZI + 1), LANES), jnp.int32),
            moves,
            moves,
            pltpu.VMEM((3, AZI, QUADS, LANES), F32),
            pltpu.VMEM((3, AZI, QUADS, LANES), F32),
            pltpu.VMEM((AZI, 4, LANES), F32),
            pltpu.VMEM((AZI, 4, LANES), F32),
            pltpu.VMEM((RAD, AZI // 2, LANES), F32),
            pltpu.VMEM((RAD, AZI // 2, LANES), F32),
            pltpu.VMEM((2, 16, LANES), F32),
            pltpu.VMEM((RAD, 16, LANES), F32),
            pltpu.VMEM((LANES, LANES), F32),
            single,
            single,
            pltpu.VMEM((8, NR, NR), jnp.bfloat16),
            pltpu.VMEM((256, 128), F32),
            pltpu.VMEM((2, 128, 256), jnp.bfloat16),
            pltpu.VMEM((256, 128), F32),
            pltpu.VMEM((256, 256), F32),
            pltpu.VMEM((2, 256, 256), jnp.bfloat16),
            pltpu.SMEM((SLAB,), jnp.int32),
            pltpu.SMEM((SLAB,), F32),
            pltpu.SemaphoreType.DMA((11,)),
            pltpu.SemaphoreType.DMA((8,)),
            pltpu.SemaphoreType.DMA((8,)),
            pltpu.SemaphoreType.DMA((7,)),
            pltpu.SemaphoreType.DMA((7,)),
        ],
        compiler_params=pltpu.CompilerParams(
            collective_id=0, has_side_effects=True, vmem_limit_bytes=40 * 1024 * 1024
        ),
    )(
        *[
            pltpu.with_memory_space_constraint(value, pltpu.HBM)
            for value in (
                density, radial_velocity, azimuthal_velocity, cycle_shift, remainder, kernel,
                *[jnp.asarray(table) for table in tables()],
            )
        ]
    )
    *fields, potential = pl.pallas_call(
        unload,
        name="unload",
        out_shape=shapes,
        in_specs=[whole] * 4,
        out_specs=[pl.BlockSpec(memory_space=pl.ANY)] * 4,
        scratch_shapes=[pltpu.SemaphoreType.DMA((4,))],
        compiler_params=pltpu.CompilerParams(vmem_limit_bytes=8 * 1024 * 1024),
    )(*results)
    return *fields, potential.reshape(1, NPHI)


def solution(mesh):
    field = P(None, "rad", "azi")
    both = P(("rad", "azi"), None)
    return jax.shard_map(
        step,
        mesh=mesh,
        in_specs=(field, field, field, P("rad"), P("rad"), P(("rad", "azi"), None, None)),
        out_specs=(field, field, field, both),
        check_vma=False,
    )
```

```python
import numpy as np

import jax
import jax.numpy as jnp
from jax import lax
from jax.experimental import pallas as pl
from jax.experimental.pallas import tpu as pltpu
from jax.sharding import PartitionSpec as P

NZ = 4
NPHI = 16384
MODES = 2048
NR = 256
RAD = 8
AZI = 32
SLAB = NR // RAD
SEG = NPHI // AZI
LANES = 128
QUADS = SEG // LANES
MEMBERS = 3 * NZ
WORDS = MEMBERS // 2
ROWS = WORDS * QUADS
FIRST_MOVES = 9
CODES = 32767
OCTAVES = 28.0
TOP = 4.0
EXT_R = SLAB + 8
EXT_P = SEG + LANES
RADIAL_COURANT = 0.3
VISCOSITY = 0.08
HIGHEST = lax.Precision.HIGHEST
F32 = jnp.float32
MESH = pl.DeviceIdType.MESH


def tables():
    n = np.arange(128)
    turn = 2.0 * np.pi / 128 * (np.outer(n, n) % 128)
    first = np.concatenate([np.cos(turn), -np.sin(turn)], axis=0)
    last = np.concatenate([np.cos(turn), -np.sin(turn)], axis=1)
    small = 2.0 * np.pi / NPHI * np.outer(n, n)
    twiddle = np.concatenate([np.cos(small), np.sin(small)], axis=0)
    col = np.arange(256)
    half, ring, part = col // 128, col % 128 // 16, col % 2
    phi = 2.0 * np.pi / 128 * (np.outer(n, 2 * ring + half) % 128)
    cos, sin = np.cos(phi), np.sin(phi)
    real = part == 0
    straight = np.concatenate([np.where(real, cos, -sin), np.where(real, sin, cos)], axis=0)
    real = real[:, None]
    back = np.concatenate(
        [np.where(real, cos.T, -sin.T), np.where(real, sin.T, cos.T)], axis=1
    )
    pairs = []
    for table in (last, back):
        high = table.astype(jnp.bfloat16)
        pairs.append(np.stack([high, (table - high.astype(np.float64)).astype(jnp.bfloat16)]))
    return [t.astype(np.float32) for t in (first, twiddle, straight)] + pairs


def dot(left, right):
    return jnp.dot(left, right, precision=HIGHEST, preferred_element_type=F32)


def halves_of(value):
    high = value.astype(jnp.bfloat16)
    return high, (value - high.astype(F32)).astype(jnp.bfloat16)


def dot_split(left, right):
    def part(a, b):
        return jnp.dot(a, b, preferred_element_type=F32)

    return part(left[0], right[0]) + (part(left[0], right[1]) + part(left[1], right[0]))


def iota(shape, axis):
    return lax.broadcasted_iota(jnp.int32, shape, axis)


def wide(value, count):
    return jnp.concatenate([value] * count, axis=1)


def cubic_weights(remainder):
    moved = -remainder
    w_next = moved * (moved + 1.0) * (moved + 2.0) / 6.0
    w_here = -(moved - 1.0) * (moved + 1.0) * (moved + 2.0) / 2.0
    w_prev = (moved - 1.0) * moved * (moved + 2.0) / 2.0
    w_prev_two = -(moved - 1.0) * moved * (moved + 1.0) / 6.0
    return w_next, w_here, w_prev, w_prev_two


def encode(value):
    level = (jnp.log(jnp.abs(value)) * (1.0 / np.log(2.0)) - TOP) * (CODES / OCTAVES) + (CODES + 0.5)
    code = jnp.clip(level, 0.0, CODES + 0.5).astype(jnp.int32)
    return jnp.where(value < 0, -code, code)


def decode(code):
    level = (jnp.abs(code) - CODES).astype(F32) * (OCTAVES / CODES) + TOP
    size = jnp.where(code == 0, 0.0, jnp.exp(level * np.log(2.0)))
    return jnp.where(code < 0, -size, size)


def rates(get, z, rows, coeffs):
    courant, coriolis, epicycle = coeffs
    below, above = max(z - 1, 0), min(z + 1, NZ - 1)
    center, ahead, rad_diff, azi_diff, spread = [], [], [], [], []
    for c in range(3):
        whole = get(c, z)
        inner = pltpu.roll(whole, 1, 0)[:rows]
        outer = pltpu.roll(whole, EXT_R - 1, 0)[:rows]
        mid = whole[:rows]
        prev = pltpu.roll(mid, 1, 1)
        following = pltpu.roll(mid, EXT_P - 1, 1)
        center.append(mid)
        rad_diff.append(outer - inner if c < 2 else None)
        azi_diff.append(following - prev if c != 1 else None)
        total = (get(c, below)[:rows] + get(c, above)[:rows]) + (inner + outer) + (prev + following)
        spread.append(VISCOSITY * (total - 6.0 * mid))
    half = 0.5 * RADIAL_COURANT
    change = (
        spread[0] - (half * rad_diff[1] + courant * azi_diff[2]),
        spread[1] + coriolis * center[2] - half * rad_diff[0],
        spread[2] - epicycle * center[1] - courant * azi_diff[0],
    )
    return change, center


def body(
    density, radial_velocity, azimuthal_velocity, shift_far, rest_far, kernel, first, twiddle, straight, last,
    back, density_out, radial_out, azimuthal_out, potential,
    ext, sect, coef, weight, row_send, row_in, tile_in, col_send, col_in, move_out, cycle_in, cycle_out,
    move_in, surf_out, surf_in, spec_out, spec_in, modes_out, modes_in, pot_out, pot_in, lines, back_out,
    back_in, kern, t_first, t_last, t_twiddle, t_straight, t_back,
    shift, rest, local_sem, halo_send, halo_recv, send_sem, recv_sem,
):
    rad, azi = lax.axis_index("rad"), lax.axis_index("azi")
    outer, inner = lax.rem(rad + 1, RAD), lax.rem(rad + RAD - 1, RAD)
    right, left = lax.rem(azi + 1, AZI), lax.rem(azi + AZI - 1, AZI)

    loads = [
        pltpu.make_async_copy(src, ext.at[pl.ds(NZ * c, NZ), pl.ds(0, SLAB), pl.ds(0, SEG)], local_sem.at[c])
        for c, src in enumerate((density, radial_velocity, azimuthal_velocity))
    ]
    for n, (src, dst) in enumerate(
        (
            (first, t_first), (twiddle, t_twiddle), (straight, t_straight),
            (kernel, kern), (back, t_back), (last, t_last), (shift_far, shift), (rest_far, rest),
        )
    ):
        loads.append(pltpu.make_async_copy(src, dst, local_sem.at[3 + n]))
    for load in loads:
        load.start()

    col_in[...] = jnp.zeros(col_in.shape, F32)
    barrier = pltpu.get_barrier_semaphore()

    def greet_azi(step, carry):
        pl.semaphore_signal(
            barrier, inc=1, device_id={"rad": rad, "azi": lax.rem(azi + step, AZI)}, device_id_type=MESH
        )
        return carry

    def greet_rad(step, carry):
        pl.semaphore_signal(
            barrier, inc=1, device_id={"rad": lax.rem(rad + step, RAD), "azi": azi}, device_id_type=MESH
        )
        return carry

    for r_to in (outer, inner):
        for a_to in (right, left):
            pl.semaphore_signal(barrier, inc=1, device_id={"rad": r_to, "azi": a_to}, device_id_type=MESH)
    lax.fori_loop(1, AZI, greet_azi, 0)
    lax.fori_loop(1, RAD, greet_rad, 0)

    for load in loads[:3]:
        load.wait()
    for c in range(3):
        heights = [ext[NZ * c + z, pl.ds(0, SLAB), pl.ds(0, SEG)] for z in range(NZ)]
        total = (heights[0] + heights[1]) + (heights[2] + heights[3])
        for n in range(SLAB):
            for quad in range(QUADS):
                surf_out[c, n, quad, :] = total[n, LANES * quad : LANES * (quad + 1)]

    lane_tile = iota((SLAB, LANES), 1)
    mixed = []
    for m in range(MEMBERS):
        low = ext[m, pl.ds(0, SLAB), pl.ds(0, LANES)]
        high = ext[m, pl.ds(0, SLAB), pl.ds(SEG - LANES, LANES)]
        edge = jnp.where(lane_tile < LANES // 2, low, high)
        mixed.append(edge)
        for n, at in enumerate((SLAB - 2, 0)):
            row_send[n, pl.ds(2 * m, 2), pl.ds(0, SEG)] = ext[m, pl.ds(at, 2), pl.ds(0, SEG)]
            row_send[n, pl.ds(2 * m, 2), pl.ds(SEG, LANES)] = edge[at : at + 2]
    columns = jnp.concatenate(mixed, axis=0).T
    col_send[0] = columns[LANES - 8 :]
    col_send[1] = columns[:8]


    finish = []

    def to_azi(n, src, dst, step):
        return pltpu.make_async_remote_copy(
            src_ref=src, dst_ref=dst, send_sem=send_sem.at[n], recv_sem=recv_sem.at[n],
            device_id={"rad": rad, "azi": lax.rem(azi + step, AZI)}, device_id_type=MESH,
        )

    def to_rad(n, src, dst, step):
        return pltpu.make_async_remote_copy(
            src_ref=src, dst_ref=dst, send_sem=send_sem.at[n], recv_sem=recv_sem.at[n],
            device_id={"rad": lax.rem(rad + step, RAD), "azi": azi}, device_id_type=MESH,
        )

    def every(count, make, begin=1, end=None):
        def one(step, carry):
            make(lax.rem(step + count // 2 - 2, count - 1) + 1).start()
            return carry

        lax.fori_loop(begin, end or count, one, 0)

    def rows(index, size=ROWS):
        return pl.ds(pl.multiple_of(index * size, 8), size)

    def wait_all(n, ref, sem):
        pltpu.make_async_copy(ref, ref, sem.at[n]).wait()

    def later(n, ref):
        finish.append(lambda: wait_all(n, ref, send_sem))

    def target(step):
        return lax.rem(azi + step, AZI)

    def ring(step):
        return lax.rem(rad + step, RAD)

    pl.semaphore_wait(barrier, AZI - 1 + RAD - 1 + 4)

    every(AZI, lambda s: to_azi(0, surf_out.at[:, target(s)], surf_in.at[:, azi], s))
    later(0, surf_in.at[:, pl.ds(1, AZI - 1)])
    for c in range(3):
        surf_in[c, azi] = surf_out[c, azi]

    def halo(n, src, dst, r_to, a_to):
        return pltpu.make_async_remote_copy(
            src_ref=src, dst_ref=dst, send_sem=halo_send.at[n], recv_sem=halo_recv.at[n],
            device_id={"rad": r_to, "azi": a_to}, device_id_type=MESH,
        )

    plain, corner = pl.ds(0, SEG), pl.ds(SEG, LANES)
    halos = [
        halo(0, row_send.at[0, :, plain], row_in.at[0], outer, azi),
        halo(1, row_send.at[1, :, plain], row_in.at[1], inner, azi),
        halo(2, col_send.at[0], col_in.at[pl.ds(LANES - 8, 8)], rad, right),
        halo(3, col_send.at[1], col_in.at[pl.ds(0, 8)], rad, left),
        halo(4, row_send.at[0, :, corner], tile_in.at[0], outer, right),
        halo(5, row_send.at[0, :, corner], tile_in.at[1], outer, left),
        halo(6, row_send.at[1, :, corner], tile_in.at[2], inner, right),
        halo(7, row_send.at[1, :, corner], tile_in.at[3], inner, left),
    ]
    for one in halos:
        one.start()
    finish += [one.wait_send for one in halos]

    row = iota((EXT_R, LANES), 0)
    cycle = SLAB * rad + jnp.where(row < SLAB + 4, row, row - EXT_R)
    radius = 1.0 + 4.0 * (cycle.astype(F32) + 0.5) / NR
    steep = 1.0 / (radius * jnp.sqrt(radius))
    coef[0] = 0.15 / radius
    coef[1] = 0.2 * steep
    coef[2] = 0.05 * steep
    for load in loads[9:]:
        load.wait()
    block_row = iota((8, LANES), 0)
    for block in range(SLAB // 8):
        fraction = jnp.zeros((8, LANES), F32)
        for n in range(8):
            fraction = jnp.where(block_row == n, rest[8 * block + n], fraction)
        for n, value in enumerate(cubic_weights(fraction)):
            weight[n, pl.ds(8 * block, 8), :] = value
    ext[:, pl.ds(SLAB, 8), :] = jnp.zeros((MEMBERS, 8, EXT_P), F32)

    for load in loads[3:6]:
        load.wait()
    wait_all(0, surf_in.at[:, pl.ds(1, AZI - 1)], recv_sem)
    sums = jnp.concatenate([surf_in[c].reshape(128, 128) for c in range(3)], axis=1)
    halves = dot(t_first[...], sums)
    joined = []
    for c in range(3):
        turn_cos, turn_sin = t_twiddle[:128], t_twiddle[128:]
        real, imag = halves[:128, 128 * c : 128 * (c + 1)], halves[128:, 128 * c : 128 * (c + 1)]
        joined.append(
            jnp.concatenate([real * turn_cos + imag * turn_sin, imag * turn_cos - real * turn_sin], axis=1)
        )
    modes = dot(jnp.concatenate(joined, axis=0), t_straight[...])
    own = iota((384, 256), 0) % 8 == iota((384, 256), 1) // 2 % 8
    pick = (iota((48, 384), 1) // 8 == iota((48, 384), 0)).astype(F32)
    modes = dot(pick, jnp.where(own, modes, 0.0))
    note = jnp.where(iota((1, LANES), 1) % 2 == 0, shift[azi].astype(F32), rest[azi])
    for h in range(2):
        for q in range(16):
            for c in range(3):
                spec_out[16 * h + q, c, :] = modes[16 * c + q, 128 * h : 128 * (h + 1)]
            spec_out[16 * h + q, 3, :] = note[0]
    every(AZI, lambda s: to_azi(2, spec_out.at[target(s)], spec_in.at[azi], s))
    later(2, spec_in.at[pl.ds(1, AZI - 1)])
    spec_in[azi] = spec_out[azi]

    for one in halos:
        one.wait_recv()

    sides = col_in[...].T
    lane_two = iota((2, LANES), 1)
    for m in range(MEMBERS):
        ext[m, pl.ds(0, SLAB), pl.ds(SEG, LANES)] = sides[SLAB * m : SLAB * (m + 1)]
    for m in range(MEMBERS):
        pair = pl.ds(2 * m, 2)
        for n, (at, edge_at, at_edge) in enumerate(
            ((EXT_R - 2, 0, rad == 0), (SLAB, SLAB - 1, rad == RAD - 1))
        ):
            edge = ext[m, pl.ds(edge_at, 1), :]
            far = jnp.where(lane_two < LANES // 2, tile_in[2 * n + 1, pair, :], tile_in[2 * n, pair, :])
            got = jnp.concatenate([row_in[n, pair, :], far], axis=1)
            ext[m, pl.ds(at, 2), :] = jnp.where(at_edge, jnp.broadcast_to(edge, (2, EXT_P)), got)

    coeffs = [wide(coef[n], EXT_P // LANES) for n in range(3)]
    for z in range(NZ):
        change, center = rates(lambda c, zz: ext[NZ * c + zz], z, EXT_R, coeffs)
        for c in range(3):
            sect[NZ * c + z] = center[c] + change[c]
    for m in range(MEMBERS):
        top = sect[m, pl.ds(0, 1), :]
        sect[m, pl.ds(EXT_R - 1, 1), :] = jnp.where(rad == 0, top, sect[m, pl.ds(EXT_R - 1, 1), :])
        low = sect[m, pl.ds(SLAB - 1, 1), :]
        sect[m, pl.ds(SLAB, 1), :] = jnp.where(rad == RAD - 1, low, sect[m, pl.ds(SLAB, 1), :])
    coeffs = [wide(coef[n, pl.ds(0, SLAB), :], EXT_P // LANES) for n in range(3)]
    weights = [weight[n] for n in range(4)]
    lower = {}
    for z in range(NZ):
        change, center = rates(lambda c, zz: sect[NZ * c + zz], z, SLAB, coeffs)
        for c in range(3):
            m = NZ * c + z
            hydro = 0.5 * ext[m, pl.ds(0, SLAB), :] + 0.5 * (center[c] + change[c])
            ahead = pltpu.roll(hydro, EXT_P - 1, 1)
            behind = pltpu.roll(hydro, 1, 1)
            behind_two = pltpu.roll(hydro, 2, 1)
            for quad in range(QUADS):
                lanes = slice(LANES * quad, LANES * (quad + 1))
                moved = (
                    weights[0] * ahead[:, lanes] + weights[1] * hydro[:, lanes]
                    + weights[2] * behind[:, lanes] + weights[3] * behind_two[:, lanes]
                )
                code = encode(moved)
                if z % 2 == 0:
                    lower[c, quad] = code & 0xFFFF
                    continue
                words = (code << 16) | lower[c, quad]
                for block in range(SLAB // 8):
                    at = 8 * ROWS * block + WORDS * quad + 2 * c + z // 2
                    move_out[pl.ds(at, 8, stride=ROWS), :] = words[8 * block : 8 * block + 8]

    def send_moves(begin, end):
        every(AZI, lambda s: to_azi(1, move_out.at[rows(target(s))], cycle_in.at[rows(azi)], s), begin, end)

    send_moves(1, FIRST_MOVES)
    cycle_in[rows(azi), :] = move_out[rows(azi), :]

    wait_all(2, spec_in.at[pl.ds(1, AZI - 1)], recv_sem)
    tile_lane = iota((AZI // 2, LANES), 1) // 16
    parts = [spec_in[pl.ds(16 * h, 16), c, :] for h in range(2) for c in range(4)]
    for n in range(RAD):
        packed = parts[0] if n == 0 else pltpu.roll(parts[0], LANES - 16 * n, 1)
        for at in range(1, 8):
            turn = 16 * (at - n) % LANES
            packed = jnp.where(tile_lane == at, pltpu.roll(parts[at], turn, 1) if turn else parts[at], packed)
        modes_out[n] = packed
    every(RAD, lambda s: to_rad(4, modes_out.at[ring(s)], modes_in.at[rad], s))
    later(4, modes_in.at[pl.ds(1, RAD - 1)])
    send_moves(FIRST_MOVES, AZI)
    later(1, cycle_in.at[pl.ds(0, ROWS * (AZI - 1))])
    modes_in[rad] = modes_out[rad]

    shape = (16, NR)
    mode = 256 * rad + 8 * azi + iota(shape, 0) // 2
    part = iota(shape, 0) % 2
    at_cycle = iota(shape, 1)
    theta = (2.0 * np.pi / NPHI) * mode.astype(F32)
    wave_cos, wave_sin = jnp.cos(theta), jnp.sin(theta)
    double_cos, double_sin = jnp.cos(2.0 * theta), jnp.sin(2.0 * theta)
    cycle_radius = 1.0 + 4.0 * (at_cycle.astype(F32) + 0.5) / NR
    cycle_steep = 1.0 / (cycle_radius * jnp.sqrt(cycle_radius))
    courant, coriolis, epicycle = 0.3 / cycle_radius, 0.2 * cycle_steep, 0.05 * cycle_steep
    drift = courant * wave_sin
    bend = 2.0 * wave_cos - 2.0

    def times_i(value):
        return jnp.where(part == 0, -pltpu.roll(value, 15, 0), pltpu.roll(value, 1, 0))

    def neighbours(value):
        behind = jnp.where(at_cycle == 0, value, pltpu.roll(value, 1, 1))
        ahead = jnp.where(at_cycle == NR - 1, value, pltpu.roll(value, NR - 1, 1))
        return 0.5 * (ahead - behind), (ahead + behind - 2.0 * value) + bend * value

    loads[6].wait()
    wait_all(4, modes_in.at[pl.ds(1, RAD - 1)], recv_sem)
    arrived = []
    for n in range(RAD):
        arrived += [modes_in[n], pltpu.roll(modes_in[n], LANES // 2, 1)]
    arrived = jnp.concatenate(arrived, axis=0).T
    rho, ur, up, extra = [arrived[16 * c : 16 * (c + 1)] for c in range(4)]
    cycle_turn = jnp.where(part == 0, extra, pltpu.roll(extra, 1, 0)).astype(jnp.int32)
    fraction = jnp.where(part == 0, pltpu.roll(extra, 15, 0), extra)
    phase = (2.0 * np.pi / NPHI) * ((mode * cycle_turn) & (NPHI - 1)).astype(F32)
    phase_cos, phase_sin = jnp.cos(phase), jnp.sin(phase)
    w_next, w_here, w_prev, w_prev_two = cubic_weights(fraction)
    mix_real = (w_next + w_prev) * wave_cos + w_here + w_prev_two * double_cos
    mix_imag = (w_next - w_prev) * wave_sin - w_prev_two * double_sin
    turn_real = mix_real * phase_cos + mix_imag * phase_sin
    turn_imag = mix_imag * phase_cos - mix_real * phase_sin
    rho_diff, rho_spread = neighbours(rho)
    ur_diff, ur_spread = neighbours(ur)
    rho_one = rho - (RADIAL_COURANT * ur_diff + drift * times_i(up)) + VISCOSITY * rho_spread
    ur_one = ur + coriolis * up - RADIAL_COURANT * rho_diff + VISCOSITY * ur_spread
    up_one = up - epicycle * ur - drift * times_i(rho) + VISCOSITY * neighbours(up)[1]
    change = VISCOSITY * neighbours(rho_one)[1] - (
        RADIAL_COURANT * neighbours(ur_one)[0] + drift * times_i(up_one)
    )
    surface = 0.5 * rho + 0.5 * (rho_one + change)
    spectrum = (turn_real * surface + turn_imag * times_i(surface)).astype(jnp.bfloat16)

    mode_potential = jnp.zeros(shape, F32)
    for k in range(8):
        product = lax.dot_general(
            spectrum, kern[k], (((1,), (1,)), ((), ())), preferred_element_type=F32
        )
        mode_potential = jnp.where(iota(shape, 0) // 2 == k, product, mode_potential)
    for h in range(2):
        pot_out[h] = mode_potential[:, LANES * h : LANES * (h + 1)]
    every(RAD, lambda s: to_rad(5, pot_out.at[ring(s) // 4], pot_in.at[rad], s))
    later(5, pot_in.at[pl.ds(1, RAD - 1)])
    pot_in[rad] = pot_out[rad // 4]
    wait_all(1, cycle_in.at[pl.ds(0, ROWS * (AZI - 1))], recv_sem)
    cycle_in[pl.ds(ROWS * AZI, ROWS), :] = cycle_in[pl.ds(0, ROWS), :]
    my_shift = shift[azi]
    turn_rows, turn_lanes = my_shift // LANES, my_shift % LANES
    lane = iota((ROWS, LANES), 1)

    def rotated(segment):
        start = lax.rem(QUADS * segment + LANES - 1 - turn_rows + LANES, LANES) * WORDS
        here = cycle_in[pl.ds(start + WORDS, ROWS), :]
        before = cycle_in[pl.ds(start, ROWS), :]
        return pltpu.roll(jnp.where(lane < LANES - turn_lanes, here, before), turn_lanes, 1)

    def rotate_and_send(step, carry):
        step = lax.rem(step + AZI // 2 - 2, AZI - 1) + 1
        segment = target(step)
        cycle_out[rows(segment), :] = rotated(segment)
        to_azi(3, cycle_out.at[rows(segment)], move_in.at[rows(azi)], step).start()
        return carry

    lax.fori_loop(1, AZI, rotate_and_send, 0)
    later(3, move_in.at[pl.ds(0, ROWS * (AZI - 1))])
    move_in[rows(azi), :] = rotated(azi)

    wait_all(5, pot_in.at[pl.ds(1, RAD - 1)], recv_sem)
    lines[...] = pot_in[...].reshape(LANES, LANES).T
    gathered = lines[rows(lax.rem(rad, 4), SLAB), :]
    for n in range(SLAB):
        back_out[n, 0, :] = gathered[n]
    every(AZI, lambda s: to_azi(6, back_out.at[target(s)], back_in.at[azi], s))
    later(6, back_in.at[pl.ds(1, AZI - 1)])
    back_in[azi] = back_out[azi]
    wait_all(3, move_in.at[pl.ds(0, ROWS * (AZI - 1))], recv_sem)
    for c, out in enumerate((density_out, radial_out, azimuthal_out)):
        for pair in range(NZ // 2):
            for quad in range(QUADS):
                for block in range(SLAB // 8):
                    at = 8 * ROWS * block + WORDS * quad + 2 * c + pair
                    words = move_in[pl.ds(at, 8, stride=ROWS), :]
                    place = pl.ds(8 * block, 8), pl.ds(LANES * quad, LANES)
                    out[2 * pair, *place] = decode((words << 16) >> 16)
                    out[2 * pair + 1, *place] = decode(words >> 16)

    for load in loads[7:9]:
        load.wait()
    wait_all(6, back_in.at[pl.ds(1, AZI - 1)], recv_sem)
    values = back_in[:, 0, :]
    values = jnp.concatenate([values[:16], values[16:]], axis=1)
    spread = (iota((128, 16), 0) // 8 == iota((128, 16), 1)).astype(F32).astype(jnp.bfloat16)
    high, low = [jnp.dot(spread, piece, preferred_element_type=F32) for piece in halves_of(values)]
    zero_mode = (iota((128, 256), 0) == 0) & (iota((128, 256), 1) < 2)
    own = iota((128, 256), 0) % 8 == iota((128, 256), 1) // 2 % 8
    values = jnp.where(own, (high + low) * jnp.where(zero_mode, 1.0 / NPHI, 2.0 / NPHI), 0.0)
    pieces = dot_split(halves_of(values), (t_back[0], t_back[1]))
    real, imag = pieces[:, :128], pieces[:, 128:]
    turn_cos, turn_sin = t_twiddle[:128], t_twiddle[128:]
    joined = jnp.concatenate([real * turn_cos - imag * turn_sin, real * turn_sin + imag * turn_cos], axis=0)
    potential[...] = dot_split((t_last[0], t_last[1]), halves_of(joined))


    for wait in finish:
        wait()


def unload(*refs):
    pairs, sems = zip(refs[:4], refs[4:8]), refs[8]
    copies = [pltpu.make_async_copy(src, dst, sems.at[n]) for n, (src, dst) in enumerate(pairs)]
    for copy in copies:
        copy.start()
    for copy in copies:
        copy.wait()


def step(density, radial_velocity, azimuthal_velocity, cycle_shift, remainder, kernel):
    whole = pl.BlockSpec(memory_space=pltpu.VMEM)
    away = pl.BlockSpec(memory_space=pltpu.HBM)
    shapes = [jax.ShapeDtypeStruct((NZ, SLAB, SEG), F32)] * 3 + [jax.ShapeDtypeStruct((128, 128), F32)]
    moves = pltpu.VMEM((ROWS * AZI, LANES), jnp.int32)
    single = pltpu.VMEM((AZI, 1, LANES), F32)
    results = pl.pallas_call(
        body,
        name="disc_step",
        out_shape=shapes,
        in_specs=[away] * 11,
        out_specs=[whole] * 4,
        scratch_shapes=[
            pltpu.VMEM((MEMBERS, EXT_R, EXT_P), F32),
            pltpu.VMEM((MEMBERS, EXT_R, EXT_P), F32),
            pltpu.VMEM((3, EXT_R, LANES), F32),
            pltpu.VMEM((4, SLAB, LANES), F32),
            pltpu.VMEM((2, 2 * MEMBERS, EXT_P), F32),
            pltpu.VMEM((2, 2 * MEMBERS, SEG), F32),
            pltpu.VMEM((4, 2 * MEMBERS, LANES), F32),
            pltpu.VMEM((2, 8, MEMBERS * SLAB), F32),
            pltpu.VMEM((LANES, MEMBERS * SLAB), F32),
            moves,
            pltpu.VMEM((ROWS * (AZI + 1), LANES), jnp.int32),
            moves,
            moves,
            pltpu.VMEM((3, AZI, QUADS, LANES), F32),
            pltpu.VMEM((3, AZI, QUADS, LANES), F32),
            pltpu.VMEM((AZI, 4, LANES), F32),
            pltpu.VMEM((AZI, 4, LANES), F32),
            pltpu.VMEM((RAD, AZI // 2, LANES), F32),
            pltpu.VMEM((RAD, AZI // 2, LANES), F32),
            pltpu.VMEM((2, 16, LANES), F32),
            pltpu.VMEM((RAD, 16, LANES), F32),
            pltpu.VMEM((LANES, LANES), F32),
            single,
            single,
            pltpu.VMEM((8, NR, NR), jnp.bfloat16),
            pltpu.VMEM((256, 128), F32),
            pltpu.VMEM((2, 128, 256), jnp.bfloat16),
            pltpu.VMEM((256, 128), F32),
            pltpu.VMEM((256, 256), F32),
            pltpu.VMEM((2, 256, 256), jnp.bfloat16),
            pltpu.SMEM((SLAB,), jnp.int32),
            pltpu.SMEM((SLAB,), F32),
            pltpu.SemaphoreType.DMA((11,)),
            pltpu.SemaphoreType.DMA((8,)),
            pltpu.SemaphoreType.DMA((8,)),
            pltpu.SemaphoreType.DMA((7,)),
            pltpu.SemaphoreType.DMA((7,)),
        ],
        compiler_params=pltpu.CompilerParams(
            collective_id=0, has_side_effects=True, vmem_limit_bytes=40 * 1024 * 1024
        ),
    )(
        *[
            pltpu.with_memory_space_constraint(value, pltpu.HBM)
            for value in (
                density, radial_velocity, azimuthal_velocity, cycle_shift, remainder, kernel,
                *[jnp.asarray(table) for table in tables()],
            )
        ]
    )
    *fields, potential = pl.pallas_call(
        unload,
        name="unload",
        out_shape=shapes,
        in_specs=[whole] * 4,
        out_specs=[pl.BlockSpec(memory_space=pl.ANY)] * 4,
        scratch_shapes=[pltpu.SemaphoreType.DMA((4,))],
        compiler_params=pltpu.CompilerParams(vmem_limit_bytes=8 * 1024 * 1024),
    )(*results)
    return *fields, potential.reshape(1, NPHI)


def solution(mesh):
    field = P(None, "rad", "azi")
    both = P(("rad", "azi"), None)
    return jax.shard_map(
        step,
        mesh=mesh,
        in_specs=(field, field, field, P("rad"), P("rad"), P(("rad", "azi"), None, None)),
        out_specs=(field, field, field, both),
        check_vma=False,
    )
```
